32 devices in a mesh: groups: 2 (over y), seq: 4 (over z), head: 2 (over x), mp: 2 (over core).
Axes of the slice: x: 2, y: 2, z: 4, core: 2. Of those that a mesh axis runs over, the one named last changes fastest.
Arguments:
- span_order: int32 [16], P('groups'), parts along dimension 0, may hold values from 0 to 7, as said below
- queries: bfloat16 [2048, 1024], P(('groups', 'seq'), ('head', 'mp')), parts along dimension 0, may hold values from -22 to 22
- keys: bfloat16 [2048, 1024], P(('groups', 'seq'), ('head', 'mp')), parts along dimension 0, may hold values from -22 to 22
- values: bfloat16 [2048, 1024], P(('groups', 'seq'), ('head', 'mp')), parts along dimension 0, may hold values from -6 to 6
- grad_out: bfloat16 [2048, 1024], P(('groups', 'seq'), ('head', 'mp')), parts along dimension 0, may hold values from -6 to 6
Outputs:
- attended: bfloat16 [2048, 1024], P(('groups', 'seq'), ('head', 'mp')), parts along dimension 0
- grad_queries: bfloat16 [2048, 1024], P(('groups', 'seq'), ('head', 'mp')), parts along dimension 0
- grad_keys: bfloat16 [2048, 1024], P(('groups', 'seq'), ('head', 'mp')), parts along dimension 0
- grad_values: bfloat16 [2048, 1024], P(('groups', 'seq'), ('head', 'mp')), parts along dimension 0
The draws below stay inside these ranges and needn't reach their ends.
There are 2 independent parts, one for each index of `groups`. The reference program is written for one: setup_inputs(seed, part) draws one part's arguments, and reference() takes and returns one part's arrays. A program takes and returns all parts, laid end to end along the dimension named above; each array names one. Nothing has to cross between parts.
Inputs may be any that keep to these rules, and one draw needn't show every extreme that they name: span_order is a permutation; stored spans 2 s and 2 s + 1 have places p and 7 - p with p < 4.
All inputs are finite; a program needn't handle non-finite values.
Results may differ from the reference program's by a relative error of at most 0.023.
Values may be sent and summed in bfloat16 or wider, within the bound.
No kernel may reach another device: no remote copies, remote signals or barrier semaphores. Data moves between devices by JAX's collectives and lax.ppermute only.
A program may use at most 64 MiB of HBM per device.

```python
import jax
import jax.numpy as jnp
from jax import lax

HEADS = 8
HEAD_DIM = 128
SPAN = 128
NCHUNK = 8
LENGTH = 1024
N_SEQ = 4


def draw_span_order(key, part):
    half = NCHUNK // 2
    early = jax.random.permutation(jax.random.fold_in(key, 21), half).astype(jnp.int32)
    late = (NCHUNK - 1 - early).astype(jnp.int32)
    return jnp.stack([early, late], axis=1).reshape(NCHUNK).astype(jnp.int32)


def drawn(key):
    width = HEADS * HEAD_DIM
    query_base = jnp.clip(jax.random.normal(jax.random.fold_in(key, 11), (LENGTH, width), jnp.float32), -4.0, 4.0)
    key_base = jnp.clip(jax.random.normal(jax.random.fold_in(key, 12), (LENGTH, width), jnp.float32), -4.0, 4.0)
    return (query_base, key_base)


def draw_queries(key, part):
    return drawn(key)[0].astype(jnp.bfloat16)


def draw_keys(key, part):
    return drawn(key)[1].astype(jnp.bfloat16)


def shard_levels(key, extent, pieces, smallest, top_value):
    def one(dim, parts):
        heights = jax.random.uniform(jax.random.fold_in(jax.random.fold_in(key, 6), dim), (parts,), jnp.float32, smallest / len(pieces), top_value / len(pieces))
        return jnp.repeat(jnp.exp(heights), extent[dim] // parts).reshape((-1,) + (1,) * (len(extent) - dim - 1))

    loudness = one(*pieces[0])
    for cut in pieces[1:]:
        loudness = loudness * one(*cut)
    return loudness


def noise(rng, shape, deviation, most, shards=(), held_as=jnp.bfloat16):
    entries = jax.random.normal(rng, shape, jnp.float32) * deviation
    if len(shards) > 0:
        entries = shard_levels(rng, shape, shards, -0.22, 0.18) * entries
    return jnp.clip(entries, min=-most, max=most).astype(held_as)


def setup_inputs(seed: int = 0, part: int = 0) -> dict:
    arg_keys = jax.random.split(jax.random.key(seed), 6)
    part_splits = jax.random.split(jax.random.fold_in(arg_keys[5], part), 6)
    return {
        "span_order": draw_span_order(jax.random.fold_in(jax.random.fold_in(arg_keys[5], part), 71), part),
        "queries": draw_queries(jax.random.fold_in(jax.random.fold_in(arg_keys[5], part), 71), part),
        "keys": draw_keys(jax.random.fold_in(jax.random.fold_in(arg_keys[5], part), 71), part),
        "values": noise(part_splits[3], (LENGTH, HEADS * HEAD_DIM), 1.0, 6.0, ((0, 4), (1, 4))),
        "grad_out": noise(part_splits[4], (LENGTH, HEADS * HEAD_DIM), 1.0, 6.0, ((0, 4), (1, 4))),
    }


def settle(values_in):
    return lax.optimization_barrier(values_in.astype(jnp.bfloat16)).astype(jnp.float32)


def reference(span_order, queries, keys, values, grad_out):
    factor = HEAD_DIM ** -0.5
    shard_rows = 2 * SPAN
    offsets = jnp.arange(LENGTH, dtype=jnp.int32)
    key_pos = (jnp.repeat(span_order, SPAN, total_repeat_length=LENGTH) * SPAN + offsets % SPAN).astype(jnp.int32)
    key_all = keys.astype(jnp.float32).reshape(LENGTH, HEADS, HEAD_DIM)
    value_all = values.astype(jnp.float32).reshape(LENGTH, HEADS, HEAD_DIM)

    def shard_step(carry, shard_index):
        grad_k, grad_v = carry
        start_row = (shard_index * shard_rows).astype(jnp.int32)
        q_part = lax.dynamic_slice_in_dim(queries, start_row, shard_rows, 0).astype(jnp.float32).reshape(shard_rows, HEADS, HEAD_DIM)
        g_part = lax.dynamic_slice_in_dim(grad_out, start_row, shard_rows, 0).astype(jnp.float32).reshape(shard_rows, HEADS, HEAD_DIM)
        q_pos = lax.dynamic_slice_in_dim(key_pos, start_row, shard_rows, 0)
        visible = key_pos[None, None, :] <= q_pos[None, :, None]
        scores = jnp.where(visible, jnp.einsum("qhd,khd->hqk", q_part, key_all) * factor, -jnp.inf)
        row_max = jnp.max(scores, axis=2, keepdims=True)
        lse = row_max + jnp.log(jnp.sum(jnp.exp(scores - row_max), axis=2, keepdims=True))
        probs = jnp.exp(scores - lse)
        attended = jnp.einsum("hqk,khd->qhd", probs, value_all).astype(jnp.bfloat16)
        delta = jnp.sum(g_part * attended.astype(jnp.float32), axis=2)
        dprobs = jnp.einsum("qhd,khd->hqk", g_part, value_all)
        dscores = settle(probs * (dprobs - delta.T[:, :, None]))
        grad_q = (jnp.einsum("hqk,khd->qhd", dscores, key_all) * factor).astype(jnp.bfloat16)
        grad_k = grad_k + settle(jnp.einsum("hqk,qhd->khd", dscores, q_part) * factor)
        grad_v = grad_v + settle(jnp.einsum("hqk,qhd->khd", settle(probs), g_part))
        return (grad_k, grad_v), (attended, grad_q)

    zeros = jnp.zeros((LENGTH, HEADS, HEAD_DIM), jnp.float32)
    (grad_k, grad_v), (attended, grad_q) = lax.scan(shard_step, (zeros, zeros), jnp.arange(N_SEQ, dtype=jnp.int32))
    width = HEADS * HEAD_DIM
    return (attended.reshape(LENGTH, width), grad_q.reshape(LENGTH, width),
            grad_k.astype(jnp.bfloat16).reshape(LENGTH, width), grad_v.astype(jnp.bfloat16).reshape(LENGTH, width))
```

```python
import functools

import jax
import jax.numpy as jnp
from jax import lax
from jax.experimental import pallas as pl
from jax.experimental.pallas import tpu as pltpu
from jax.sharding import PartitionSpec as P

HEAD_DIM = 128
SPAN = 128


def settle(values_in):
    return lax.optimization_barrier(values_in.astype(jnp.bfloat16)).astype(jnp.float32)


def masked_scores(query_block, key_block, query_pos, key_positions, factor):
    raw = (
        jnp.einsum("qhd,khd->hqk", query_block, key_block, preferred_element_type=jnp.float32)
        * factor
    )
    return jnp.where(key_positions[None, None, :] <= query_pos[None, :, None], raw, -jnp.inf)


def split_blocks(arrays, block_rows):
    count_blocks = arrays[0].shape[0] // block_rows
    stacked = tuple(
        (member.reshape((count_blocks, block_rows) + member.shape[1:]) for member in arrays)
    )
    starts = jnp.arange(count_blocks, dtype=jnp.int32) * block_rows
    return (stacked, starts)


def gathered_per_device(span_order, queries, keys, values, grad_out):
    q_rows, k_rows, v_rows, g_rows = (queries, keys, values, grad_out)
    my_rows = q_rows.shape[0]
    heads_here = q_rows.shape[1] // HEAD_DIM
    factor = HEAD_DIM ** (-0.5)
    total_rows = span_order.shape[0] * SPAN
    offsets = jnp.arange(total_rows, dtype=jnp.int32)
    all_pos = jnp.repeat(span_order, SPAN, total_repeat_length=total_rows) * SPAN + offsets % SPAN
    my_start = lax.axis_index("seq") * my_rows
    my_pos = lax.dynamic_slice_in_dim(all_pos, my_start, my_rows)
    my_q = q_rows.reshape(my_rows, heads_here, HEAD_DIM)
    my_k = k_rows.reshape(my_rows, heads_here, HEAD_DIM)
    my_v = v_rows.reshape(my_rows, heads_here, HEAD_DIM)
    my_g = g_rows.reshape(my_rows, heads_here, HEAD_DIM)

    def key_block_rows():
        return 512

    start_state = (
        jnp.full((heads_here, my_rows), -jnp.inf, jnp.float32),
        jnp.zeros((heads_here, my_rows), jnp.float32),
        jnp.zeros((heads_here, my_rows, HEAD_DIM), jnp.float32),
    )
    carry = start_state
    block_rows = key_block_rows()
    stacked, starts = split_blocks(
        (
            lax.all_gather(k_rows, "seq", axis=0, tiled=True),
            lax.all_gather(v_rows, "seq", axis=0, tiled=True),
        ),
        block_rows,
    )

    def forward_one_block(state, item):
        key_block, value_block, block_start = item
        key3 = key_block.reshape(block_rows, heads_here, HEAD_DIM)
        value3 = value_block.reshape(block_rows, heads_here, HEAD_DIM)
        positions = lax.dynamic_slice_in_dim(all_pos, block_start, block_rows)
        row_max, weight_sum, accum = state
        scores = masked_scores(my_q, key3, my_pos, positions, factor)
        new_max = jnp.maximum(row_max, jnp.max(scores, axis=2))
        safe_max = jnp.where(jnp.isfinite(new_max), new_max, 0.0)
        weights = jnp.exp(scores - safe_max[:, :, None])
        shrink = jnp.exp(row_max - safe_max)
        weight_sum = weight_sum * shrink + jnp.sum(weights, axis=2)
        accum = accum * shrink[:, :, None] + jnp.einsum(
            "hqk,khd->hqd", weights, value3.astype(jnp.float32)
        )
        return ((new_max, weight_sum, accum), None)

    carry, unused = lax.scan(forward_one_block, carry, stacked + (starts,))
    row_max, weight_sum, accum = carry
    lse_rows = (row_max + jnp.log(weight_sum)).T
    attended3 = jnp.transpose(accum / weight_sum[:, :, None], (1, 0, 2)).astype(jnp.bfloat16)
    delta_rows = jnp.sum(my_g.astype(jnp.float32) * attended3.astype(jnp.float32), axis=2)
    lse_all, delta_all = (
        lax.all_gather(lse_rows, "seq", axis=0, tiled=True),
        lax.all_gather(delta_rows, "seq", axis=0, tiled=True),
    )

    def pair_terms(
        q_block, g_block, lse_block, delta_block, q_pos, key_block, value_block, key_positions
    ):
        scores = masked_scores(q_block, key_block, q_pos, key_positions, factor)
        probs = jnp.exp(scores - lse_block.T[:, :, None])
        dprobs = jnp.einsum(
            "qhd,khd->hqk", g_block, value_block, preferred_element_type=jnp.float32
        )
        dscores = (probs * (dprobs - delta_block.T[:, :, None])).astype(jnp.bfloat16)
        return (probs.astype(jnp.bfloat16), dscores)

    def query_part(acc_q, key3, value3, positions):
        unused, dscores = pair_terms(
            my_q, my_g, lse_rows, delta_rows, my_pos, key3, value3, positions
        )
        return acc_q + jnp.einsum("hqk,khd->hqd", dscores, key3, preferred_element_type=jnp.float32)

    def key_part(acc_kv, q3, g3, block_start):
        positions = lax.dynamic_slice_in_dim(all_pos, block_start, my_rows)
        lse_block = lax.dynamic_slice_in_dim(lse_all, block_start, my_rows, 0)
        delta_block = lax.dynamic_slice_in_dim(delta_all, block_start, my_rows, 0)
        grad_k, grad_v = acc_kv
        probs_half, dscores = pair_terms(
            q3, g3, lse_block, delta_block, positions, my_k, my_v, my_pos
        )
        grad_k = grad_k + settle(
            jnp.einsum("hqk,qhd->khd", dscores, q3, preferred_element_type=jnp.float32) * factor
        )
        grad_v = grad_v + settle(
            jnp.einsum("hqk,qhd->khd", probs_half, g3, preferred_element_type=jnp.float32)
        )
        return (grad_k, grad_v)

    zeros_q = jnp.zeros((heads_here, my_rows, HEAD_DIM), jnp.float32)
    zeros_k = jnp.zeros((my_rows, heads_here, HEAD_DIM), jnp.float32)
    carry = zeros_q
    query_block_rows = key_block_rows()
    stacked, starts = split_blocks(
        (
            lax.all_gather(k_rows, "seq", axis=0, tiled=True),
            lax.all_gather(v_rows, "seq", axis=0, tiled=True),
        ),
        query_block_rows,
    )

    def query_one_block(state, item):
        key_block, value_block, block_start = item
        positions = lax.dynamic_slice_in_dim(all_pos, block_start, query_block_rows)
        key3 = key_block.reshape(query_block_rows, heads_here, HEAD_DIM)
        value3 = value_block.reshape(query_block_rows, heads_here, HEAD_DIM)
        return (query_part(state, key3, value3, positions), None)

    carry, unused = lax.scan(query_one_block, carry, stacked + (starts,))
    grad_q_acc = carry
    carry = (zeros_k, zeros_k)
    stacked, starts = split_blocks(
        (
            lax.all_gather(q_rows, "seq", axis=0, tiled=True),
            lax.all_gather(g_rows, "seq", axis=0, tiled=True),
        ),
        my_rows,
    )

    def key_one_block(state, item):
        query_block, cotangent_block, block_start = item
        q3 = query_block.reshape(my_rows, heads_here, HEAD_DIM)
        g3 = cotangent_block.reshape(my_rows, heads_here, HEAD_DIM)
        return (key_part(state, q3, g3, block_start), None)

    carry, unused = lax.scan(key_one_block, carry, stacked + (starts,))
    grad_k_acc, grad_v_acc = carry
    attended_rows = attended3.reshape(my_rows, heads_here * HEAD_DIM)
    grad_q_rows = (
        (jnp.transpose(grad_q_acc, (1, 0, 2)) * factor)
        .astype(jnp.bfloat16)
        .reshape(my_rows, heads_here * HEAD_DIM)
    )
    grad_k_rows = grad_k_acc.astype(jnp.bfloat16).reshape(my_rows, heads_here * HEAD_DIM)
    grad_v_rows = grad_v_acc.astype(jnp.bfloat16).reshape(my_rows, heads_here * HEAD_DIM)
    return (attended_rows, grad_q_rows, grad_k_rows, grad_v_rows)


F32=jnp.float32; BF=jnp.bfloat16
NN=(((1,),(0,)),((),())); NT=(((1,),(1,)),((),()))
def dot(a,b,dims): return lax.dot_general(a,b,dims,preferred_element_type=F32)

def owner_kernel(rows, blk, order_ref, ids_ref, own, sa, sb, sc, o_own, o_a, o_b, o_c,
                 q, k, v, g, kt, vt, s, dk, dv):
    ins=(own,sa,sb,sc); outs=(o_own,o_a,o_b,o_c)
    sh=own.shape[0]//4
    per=sh//SPAN
    total=4*sh
    factor=HEAD_DIM**-0.5
    c=factor*1.4426950408889634
    place=[]
    for t in range(4):
        for e in range(per):
            p=pl.multiple_of(order_ref[ids_ref[t]*per+e]*SPAN,SPAN)
            place.append((t,e,p))
    @pl.when(ids_ref[4]==1)
    def _():
        for t,e,p in place:
            for n,dst in enumerate((q,k,v,g)):
                dst[pl.ds(p,SPAN),:]=ins[t][n*sh+e*SPAN:n*sh+(e+1)*SPAN,:]
        nb=total//blk
        for j in range(nb):
            r=slice(j*blk,(j+1)*blk)
            kt[:,r]=k[r,:].T
            vt[:,r]=v[r,:].T
        dk[...]=jnp.zeros_like(dk); dv[...]=jnp.zeros_like(dv)
        ki=lax.broadcasted_iota(jnp.int32,(blk,blk),0); qi=lax.broadcasted_iota(jnp.int32,(blk,blk),1)
        for i in range(nb):
            ri=slice(i*blk,(i+1)*blk)
            qb=q[ri,:]
            m=None
            for j in range(i+1):
                rj=slice(j*blk,(j+1)*blk)
                sj=dot(k[rj,:],qb,NT)*c
                if j==i: sj=jnp.where(ki<=qi,sj,-1e30)
                s[rj,:]=sj
                mj=jnp.max(sj,axis=0,keepdims=True)
                m=mj if m is None else jnp.maximum(m,mj)
            l=None; ot=None
            for j in range(i+1):
                rj=slice(j*blk,(j+1)*blk)
                p=jnp.exp2(s[rj,:]-m)
                s[rj,:]=p
                lj=jnp.sum(p,axis=0,keepdims=True)
                oj=dot(vt[:,rj],p.astype(BF),NN)
                l=lj if l is None else l+lj
                ot=oj if ot is None else ot+oj
            rinv=1.0/l
            ob=(ot*rinv).astype(BF)
            gt=g[ri,:].T.astype(F32)*rinv
            gnt=gt.astype(BF)
            delta=jnp.sum(gt*ob.astype(F32),axis=0,keepdims=True)
            dqt=None
            for j in range(i+1):
                rj=slice(j*blk,(j+1)*blk)
                dp=dot(v[rj,:],gnt,NN)
                p=s[rj,:]
                ds=(p*(dp-delta)).astype(BF)
                dv[rj,:]+=dot(p.astype(BF),gnt,NT)
                dk[rj,:]+=dot(ds,qb,NN)
                dj=dot(kt[:,rj],ds,NN)
                dqt=dj if dqt is None else dqt+dj
            q[ri,:]=(dqt*factor).astype(BF).T
            g[ri,:]=ob.T
        for t,e,p in place:
            outs[t][0*sh+e*SPAN:0*sh+(e+1)*SPAN,:]=g[pl.ds(p,SPAN),:]
            outs[t][1*sh+e*SPAN:1*sh+(e+1)*SPAN,:]=q[pl.ds(p,SPAN),:]
            outs[t][2*sh+e*SPAN:2*sh+(e+1)*SPAN,:]=(dk[pl.ds(p,SPAN),:]*factor).astype(BF)
            outs[t][3*sh+e*SPAN:3*sh+(e+1)*SPAN,:]=dv[pl.ds(p,SPAN),:].astype(BF)

def owner_call(order, ids, own, sa, sb, sc, blk=256):
    sh=own.shape[0]//4; total=4*sh
    vm=pl.BlockSpec(memory_space=pltpu.VMEM); sm=pl.BlockSpec(memory_space=pltpu.SMEM)
    return pl.pallas_call(
        functools.partial(owner_kernel,total,blk),
        out_shape=tuple(jax.ShapeDtypeStruct(own.shape,BF) for _ in range(4)),
        in_specs=[sm,sm,vm,vm,vm,vm], out_specs=(vm,)*4,
        scratch_shapes=[pltpu.VMEM((total,HEAD_DIM),BF)]*4+[pltpu.VMEM((HEAD_DIM,total),BF)]*2+
            [pltpu.VMEM((total,blk),F32)]+[pltpu.VMEM((total,HEAD_DIM),F32)]*2,
        compiler_params=pltpu.CompilerParams(vmem_limit_bytes=32<<20),
        name="owner",
    )(order,ids,own,sa,sb,sc)


def pack_kernel(side_ref, q, k, v, g, near, far):
    sh = q.shape[0]
    for s in range(2):
        @pl.when(side_ref[0] == s)
        def _():
            for n, src in enumerate((q, k, v, g)):
                near[n * sh:(n + 1) * sh, :] = src[:, s * HEAD_DIM:(s + 1) * HEAD_DIM]
                far[n * sh:(n + 1) * sh, :] = src[:, (1 - s) * HEAD_DIM:(2 - s) * HEAD_DIM]


def unpack_kernel(side_ref, own, ra, rb, rc, *outs):
    sh = outs[0].shape[0]
    for s in range(2):
        for owner in range(2):
            @pl.when((side_ref[0] == s) & (side_ref[1] == owner))
            def _():
                near, far = (own, rb) if owner else (ra, rc)
                for n, dst in enumerate(outs):
                    dst[:, s * HEAD_DIM:(s + 1) * HEAD_DIM] = near[n * sh:(n + 1) * sh, :]
                    dst[:, (1 - s) * HEAD_DIM:(2 - s) * HEAD_DIM] = far[n * sh:(n + 1) * sh, :]


def owned_per_device(span_order, queries, keys, values, grad_out):
    rows = queries.shape[0]
    me = lax.axis_index("seq")
    side = jnp.where(me < 2, 0, 1)
    owner = jnp.where((me == 1) | (me == 2), 1, 0)
    near_outer = 3 * side
    ids = jnp.stack([me, near_outer, 3 - me, 3 - near_outer, owner]).astype(jnp.int32)
    flags = jnp.stack([side, owner]).astype(jnp.int32)
    vm = pl.BlockSpec(memory_space=pltpu.VMEM)
    sm = pl.BlockSpec(memory_space=pltpu.SMEM)
    near, far = pl.pallas_call(
        pack_kernel,
        out_shape=(jax.ShapeDtypeStruct((4 * rows, HEAD_DIM), BF),) * 2,
        in_specs=[sm] + [vm] * 4,
        out_specs=(vm, vm),
        name="pack",
    )(flags, queries, keys, values, grad_out)
    go = lambda x, pairs: lax.ppermute(x, "seq", pairs)
    ga = go(near, [(0, 1), (3, 2)])
    gb = go(far, [(1, 2), (2, 1)])
    gc = go(far, [(0, 2), (3, 1)])
    own, to_a, to_b, to_c = owner_call(span_order, ids, near, ga, gb, gc, blk=512)
    rb = go(to_b, [(1, 2), (2, 1)])
    rc = go(to_c, [(1, 3), (2, 0)])
    ra = go(to_a, [(1, 0), (2, 3)])
    return pl.pallas_call(
        unpack_kernel,
        out_shape=(jax.ShapeDtypeStruct(queries.shape, BF),) * 4,
        in_specs=[sm] + [vm] * 4,
        out_specs=(vm,) * 4,
        name="unpack",
    )(flags, own, ra, rb, rc)


def solution(mesh):
    rows_columns = P(("groups", "seq"), ("head", "mp"))

    def run(span_order, queries, keys, values, grad_out):
        heads_here = queries.shape[1] // HEAD_DIM // (mesh.shape["head"] * mesh.shape["mp"])
        small = mesh.shape["seq"] == 4 and heads_here == 2
        return jax.shard_map(
            owned_per_device if small else gathered_per_device,
            mesh=mesh,
            in_specs=(P("groups"),) + (rows_columns,) * 4,
            out_specs=(rows_columns,) * 4,
            check_vma=False,
        )(span_order, queries, keys, values, grad_out)

    return run
```

```python
import functools

import jax
import jax.numpy as jnp
from jax import lax
from jax.experimental import pallas as pl
from jax.experimental.pallas import tpu as pltpu
from jax.sharding import PartitionSpec as P

HEAD_DIM = 128
SPAN = 128


def settle(values_in):
    return lax.optimization_barrier(values_in.astype(jnp.bfloat16)).astype(jnp.float32)


def masked_scores(query_block, key_block, query_pos, key_positions, factor):
    raw = (
        jnp.einsum("qhd,khd->hqk", query_block, key_block, preferred_element_type=jnp.float32)
        * factor
    )
    return jnp.where(key_positions[None, None, :] <= query_pos[None, :, None], raw, -jnp.inf)


def split_blocks(arrays, block_rows):
    count_blocks = arrays[0].shape[0] // block_rows
    stacked = tuple(
        (member.reshape((count_blocks, block_rows) + member.shape[1:]) for member in arrays)
    )
    starts = jnp.arange(count_blocks, dtype=jnp.int32) * block_rows
    return (stacked, starts)


def gathered_per_device(span_order, queries, keys, values, grad_out):
    q_rows, k_rows, v_rows, g_rows = (queries, keys, values, grad_out)
    my_rows = q_rows.shape[0]
    heads_here = q_rows.shape[1] // HEAD_DIM
    factor = HEAD_DIM ** (-0.5)
    total_rows = span_order.shape[0] * SPAN
    offsets = jnp.arange(total_rows, dtype=jnp.int32)
    all_pos = jnp.repeat(span_order, SPAN, total_repeat_length=total_rows) * SPAN + offsets % SPAN
    my_start = lax.axis_index("seq") * my_rows
    my_pos = lax.dynamic_slice_in_dim(all_pos, my_start, my_rows)
    my_q = q_rows.reshape(my_rows, heads_here, HEAD_DIM)
    my_k = k_rows.reshape(my_rows, heads_here, HEAD_DIM)
    my_v = v_rows.reshape(my_rows, heads_here, HEAD_DIM)
    my_g = g_rows.reshape(my_rows, heads_here, HEAD_DIM)

    def key_block_rows():
        return 512

    start_state = (
        jnp.full((heads_here, my_rows), -jnp.inf, jnp.float32),
        jnp.zeros((heads_here, my_rows), jnp.float32),
        jnp.zeros((heads_here, my_rows, HEAD_DIM), jnp.float32),
    )
    carry = start_state
    block_rows = key_block_rows()
    stacked, starts = split_blocks(
        (
            lax.all_gather(k_rows, "seq", axis=0, tiled=True),
            lax.all_gather(v_rows, "seq", axis=0, tiled=True),
        ),
        block_rows,
    )

    def forward_one_block(state, item):
        key_block, value_block, block_start = item
        key3 = key_block.reshape(block_rows, heads_here, HEAD_DIM)
        value3 = value_block.reshape(block_rows, heads_here, HEAD_DIM)
        positions = lax.dynamic_slice_in_dim(all_pos, block_start, block_rows)
        row_max, weight_sum, accum = state
        scores = masked_scores(my_q, key3, my_pos, positions, factor)
        new_max = jnp.maximum(row_max, jnp.max(scores, axis=2))
        safe_max = jnp.where(jnp.isfinite(new_max), new_max, 0.0)
        weights = jnp.exp(scores - safe_max[:, :, None])
        shrink = jnp.exp(row_max - safe_max)
        weight_sum = weight_sum * shrink + jnp.sum(weights, axis=2)
        accum = accum * shrink[:, :, None] + jnp.einsum(
            "hqk,khd->hqd", weights, value3.astype(jnp.float32)
        )
        return ((new_max, weight_sum, accum), None)

    carry, unused = lax.scan(forward_one_block, carry, stacked + (starts,))
    row_max, weight_sum, accum = carry
    lse_rows = (row_max + jnp.log(weight_sum)).T
    attended3 = jnp.transpose(accum / weight_sum[:, :, None], (1, 0, 2)).astype(jnp.bfloat16)
    delta_rows = jnp.sum(my_g.astype(jnp.float32) * attended3.astype(jnp.float32), axis=2)
    lse_all, delta_all = (
        lax.all_gather(lse_rows, "seq", axis=0, tiled=True),
        lax.all_gather(delta_rows, "seq", axis=0, tiled=True),
    )

    def pair_terms(
        q_block, g_block, lse_block, delta_block, q_pos, key_block, value_block, key_positions
    ):
        scores = masked_scores(q_block, key_block, q_pos, key_positions, factor)
        probs = jnp.exp(scores - lse_block.T[:, :, None])
        dprobs = jnp.einsum(
            "qhd,khd->hqk", g_block, value_block, preferred_element_type=jnp.float32
        )
        dscores = (probs * (dprobs - delta_block.T[:, :, None])).astype(jnp.bfloat16)
        return (probs.astype(jnp.bfloat16), dscores)

    def query_part(acc_q, key3, value3, positions):
        unused, dscores = pair_terms(
            my_q, my_g, lse_rows, delta_rows, my_pos, key3, value3, positions
        )
        return acc_q + jnp.einsum("hqk,khd->hqd", dscores, key3, preferred_element_type=jnp.float32)

    def key_part(acc_kv, q3, g3, block_start):
        positions = lax.dynamic_slice_in_dim(all_pos, block_start, my_rows)
        lse_block = lax.dynamic_slice_in_dim(lse_all, block_start, my_rows, 0)
        delta_block = lax.dynamic_slice_in_dim(delta_all, block_start, my_rows, 0)
        grad_k, grad_v = acc_kv
        probs_half, dscores = pair_terms(
            q3, g3, lse_block, delta_block, positions, my_k, my_v, my_pos
        )
        grad_k = grad_k + settle(
            jnp.einsum("hqk,qhd->khd", dscores, q3, preferred_element_type=jnp.float32) * factor
        )
        grad_v = grad_v + settle(
            jnp.einsum("hqk,qhd->khd", probs_half, g3, preferred_element_type=jnp.float32)
        )
        return (grad_k, grad_v)

    zeros_q = jnp.zeros((heads_here, my_rows, HEAD_DIM), jnp.float32)
    zeros_k = jnp.zeros((my_rows, heads_here, HEAD_DIM), jnp.float32)
    carry = zeros_q
    query_block_rows = key_block_rows()
    stacked, starts = split_blocks(
        (
            lax.all_gather(k_rows, "seq", axis=0, tiled=True),
            lax.all_gather(v_rows, "seq", axis=0, tiled=True),
        ),
        query_block_rows,
    )

    def query_one_block(state, item):
        key_block, value_block, block_start = item
        positions = lax.dynamic_slice_in_dim(all_pos, block_start, query_block_rows)
        key3 = key_block.reshape(query_block_rows, heads_here, HEAD_DIM)
        value3 = value_block.reshape(query_block_rows, heads_here, HEAD_DIM)
        return (query_part(state, key3, value3, positions), None)

    carry, unused = lax.scan(query_one_block, carry, stacked + (starts,))
    grad_q_acc = carry
    carry = (zeros_k, zeros_k)
    stacked, starts = split_blocks(
        (
            lax.all_gather(q_rows, "seq", axis=0, tiled=True),
            lax.all_gather(g_rows, "seq", axis=0, tiled=True),
        ),
        my_rows,
    )

    def key_one_block(state, item):
        query_block, cotangent_block, block_start = item
        q3 = query_block.reshape(my_rows, heads_here, HEAD_DIM)
        g3 = cotangent_block.reshape(my_rows, heads_here, HEAD_DIM)
        return (key_part(state, q3, g3, block_start), None)

    carry, unused = lax.scan(key_one_block, carry, stacked + (starts,))
    grad_k_acc, grad_v_acc = carry
    attended_rows = attended3.reshape(my_rows, heads_here * HEAD_DIM)
    grad_q_rows = (
        (jnp.transpose(grad_q_acc, (1, 0, 2)) * factor)
        .astype(jnp.bfloat16)
        .reshape(my_rows, heads_here * HEAD_DIM)
    )
    grad_k_rows = grad_k_acc.astype(jnp.bfloat16).reshape(my_rows, heads_here * HEAD_DIM)
    grad_v_rows = grad_v_acc.astype(jnp.bfloat16).reshape(my_rows, heads_here * HEAD_DIM)
    return (attended_rows, grad_q_rows, grad_k_rows, grad_v_rows)


F32=jnp.float32; BF=jnp.bfloat16
NN=(((1,),(0,)),((),())); NT=(((1,),(1,)),((),()))
def dot(a,b,dims): return lax.dot_general(a,b,dims,preferred_element_type=F32)

def owner_kernel(rows, blk, order_ref, own, sc, sb, sa, o_own, o_c, o_b, o_a,
                 q, k, v, g, kt, vt, s, dk, dv):
    ins=(own,sa,sb,sc); outs=(o_own,o_a,o_b,o_c)
    sh=own.shape[0]//4
    per=sh//SPAN
    total=4*sh
    factor=HEAD_DIM**-0.5
    c=factor*1.4426950408889634
    _, _, held, ids = place_here()
    place=[]
    for t in range(4):
        for e in range(per):
            p=pl.multiple_of(order_ref[ids[t]*per+e]*SPAN,SPAN)
            place.append((t,e,p))
    @pl.when(held)
    def _():
        for t,e,p in place:
            for n,dst in enumerate((q,k,v,g)):
                dst[pl.ds(p,SPAN),:]=ins[t][n*sh+e*SPAN:n*sh+(e+1)*SPAN,:]
        nb=total//blk
        for j in range(nb):
            r=slice(j*blk,(j+1)*blk)
            kt[:,r]=k[r,:].T
            vt[:,r]=v[r,:].T
        dk[...]=jnp.zeros_like(dk); dv[...]=jnp.zeros_like(dv)
        ki=lax.broadcasted_iota(jnp.int32,(blk,blk),0); qi=lax.broadcasted_iota(jnp.int32,(blk,blk),1)
        for i in range(nb):
            ri=slice(i*blk,(i+1)*blk)
            qb=q[ri,:]
            m=None
            for j in range(i+1):
                rj=slice(j*blk,(j+1)*blk)
                sj=dot(k[rj,:],qb,NT)*c
                if j==i: sj=jnp.where(ki<=qi,sj,-1e30)
                s[rj,:]=sj
                mj=jnp.max(sj,axis=0,keepdims=True)
                m=mj if m is None else jnp.maximum(m,mj)
            l=None; ot=None
            for j in range(i+1):
                rj=slice(j*blk,(j+1)*blk)
                p=jnp.exp2(s[rj,:]-m)
                s[rj,:]=p
                lj=jnp.sum(p,axis=0,keepdims=True)
                oj=dot(vt[:,rj],p.astype(BF),NN)
                l=lj if l is None else l+lj
                ot=oj if ot is None else ot+oj
            rinv=1.0/l
            ob=(ot*rinv).astype(BF)
            gt=g[ri,:].T.astype(F32)*rinv
            gnt=gt.astype(BF)
            delta=jnp.sum(gt*ob.astype(F32),axis=0,keepdims=True)
            dqt=None
            for j in range(i+1):
                rj=slice(j*blk,(j+1)*blk)
                dp=dot(v[rj,:],gnt,NN)
                p=s[rj,:]
                ds=(p*(dp-delta)).astype(BF)
                dv[rj,:]+=dot(p.astype(BF),gnt,NT)
                dk[rj,:]+=dot(ds,qb,NN)
                dj=dot(kt[:,rj],ds,NN)
                dqt=dj if dqt is None else dqt+dj
            q[ri,:]=(dqt*factor).astype(BF).T
            g[ri,:]=ob.T
        for t,e,p in place:
            outs[t][0*sh+e*SPAN:0*sh+(e+1)*SPAN,:]=g[pl.ds(p,SPAN),:]
            outs[t][1*sh+e*SPAN:1*sh+(e+1)*SPAN,:]=q[pl.ds(p,SPAN),:]
            outs[t][2*sh+e*SPAN:2*sh+(e+1)*SPAN,:]=(dk[pl.ds(p,SPAN),:]*factor).astype(BF)
            outs[t][3*sh+e*SPAN:3*sh+(e+1)*SPAN,:]=dv[pl.ds(p,SPAN),:].astype(BF)

def owner_call(order, own, sa, sb, sc, blk=256):
    sh=own.shape[0]//4; total=4*sh
    vm=pl.BlockSpec(memory_space=pltpu.VMEM); sm=pl.BlockSpec(memory_space=pltpu.SMEM)
    return pl.pallas_call(
        functools.partial(owner_kernel,total,blk),
        out_shape=tuple(pltpu.VMEM(own.shape,BF) for _ in range(4)),
        in_specs=[sm,vm,vm,vm,vm], out_specs=(vm,)*4,
        scratch_shapes=[pltpu.VMEM((total,HEAD_DIM),BF)]*4+[pltpu.VMEM((HEAD_DIM,total),BF)]*2+
            [pltpu.VMEM((total,blk),F32)]+[pltpu.VMEM((total,HEAD_DIM),F32)]*2,
        compiler_params=pltpu.CompilerParams(vmem_limit_bytes=32<<20),
        name="owner",
    )(order,own,sa,sb,sc)


def place_here():
    me = lax.axis_index("seq")
    side = lax.div(me, 2)
    owner = (me == 1) | (me == 2)
    outer = 3 * side
    return me, side, owner, (me, outer, 3 - me, 3 - outer)


def columns(half):
    return pl.ds(pl.multiple_of(half * HEAD_DIM, HEAD_DIM), HEAD_DIM)


def run_copies(copies):
    for one in copies:
        one.start()
    for one in copies:
        one.wait()


def pack_kernel(q, k, v, g, near, far, sem):
    sh = q.shape[0]
    _, side, _, _ = place_here()
    run_copies([
        pltpu.make_async_copy(src.at[:, columns(half)], dst.at[n * sh:(n + 1) * sh, :], sem.at[m, n])
        for m, (dst, half) in enumerate(((far, 1 - side), (near, side)))
        for n, src in enumerate((q, k, v, g))
    ])


def unpack_kernel(own, ra, rb, rc, *refs):
    outs, sem = refs[:4], refs[4]
    sh = outs[0].shape[0]
    _, side, owner, _ = place_here()
    for held in (True, False):
        @pl.when(owner == held)
        def _():
            near, far = (own, rb) if held else (ra, rc)
            run_copies([
                pltpu.make_async_copy(src.at[n * sh:(n + 1) * sh, :], dst.at[:, columns(half)], sem.at[m, n])
                for m, (src, half) in enumerate(((near, side), (far, 1 - side)))
                for n, dst in enumerate(outs)
            ])


def owned_per_device(span_order, queries, keys, values, grad_out):
    rows = queries.shape[0]
    anywhere = pl.BlockSpec(memory_space=pl.ANY)
    vm = pl.BlockSpec(memory_space=pltpu.VMEM)
    near, far = pl.pallas_call(
        pack_kernel,
        out_shape=(pltpu.VMEM((4 * rows, HEAD_DIM), BF),) * 2,
        in_specs=[anywhere] * 4,
        out_specs=(vm,) * 2,
        scratch_shapes=[pltpu.SemaphoreType.DMA((2, 4))],
        name="pack",
    )(queries, keys, values, grad_out)
    go = lambda x, pairs: lax.ppermute(x, "seq", pairs)
    ga = go(near, [(0, 1), (3, 2)])
    gb = go(far, [(1, 2), (2, 1)])
    gc = go(far, [(0, 2), (3, 1)])
    own, to_c, to_b, to_a = owner_call(span_order, near, gc, gb, ga, blk=512)
    rb = go(to_b, [(1, 2), (2, 1)])
    rc = go(to_c, [(1, 3), (2, 0)])
    ra = go(to_a, [(1, 0), (2, 3)])
    return pl.pallas_call(
        unpack_kernel,
        out_shape=(jax.ShapeDtypeStruct(queries.shape, BF),) * 4,
        in_specs=[vm] * 4,
        out_specs=(anywhere,) * 4,
        scratch_shapes=[pltpu.SemaphoreType.DMA((2, 4))],
        name="unpack",
    )(*(pltpu.with_memory_space_constraint(x, pltpu.VMEM) for x in (own, ra, rb, rc)))


def solution(mesh):
    rows_columns = P(("groups", "seq"), ("head", "mp"))

    def run(span_order, queries, keys, values, grad_out):
        heads_here = queries.shape[1] // HEAD_DIM // (mesh.shape["head"] * mesh.shape["mp"])
        small = mesh.shape["seq"] == 4 and heads_here == 2
        return jax.shard_map(
            owned_per_device if small else gathered_per_device,
            mesh=mesh,
            in_specs=(P("groups"),) + (rows_columns,) * 4,
            out_specs=(rows_columns,) * 4,
            check_vma=False,
        )(span_order, queries, keys, values, grad_out)

    return run
```

```python
import jax
import jax.numpy as jnp
from jax import lax
from jax.experimental import pallas as pl
from jax.experimental.pallas import tpu as pltpu
from jax.sharding import PartitionSpec as P

HEAD_DIM = 128
SPAN = 128


def settle(values_in):
    return lax.optimization_barrier(values_in.astype(jnp.bfloat16)).astype(jnp.float32)


def masked_scores(query_block, key_block, query_pos, key_positions, factor):
    raw = (
        jnp.einsum("qhd,khd->hqk", query_block, key_block, preferred_element_type=jnp.float32)
        * factor
    )
    return jnp.where(key_positions[None, None, :] <= query_pos[None, :, None], raw, -jnp.inf)


def split_blocks(arrays, block_rows):
    count_blocks = arrays[0].shape[0] // block_rows
    stacked = tuple(
        (member.reshape((count_blocks, block_rows) + member.shape[1:]) for member in arrays)
    )
    starts = jnp.arange(count_blocks, dtype=jnp.int32) * block_rows
    return (stacked, starts)


def gathered_per_device(span_order, queries, keys, values, grad_out):
    q_rows, k_rows, v_rows, g_rows = (queries, keys, values, grad_out)
    my_rows = q_rows.shape[0]
    heads_here = q_rows.shape[1] // HEAD_DIM
    factor = HEAD_DIM ** (-0.5)
    total_rows = span_order.shape[0] * SPAN
    offsets = jnp.arange(total_rows, dtype=jnp.int32)
    all_pos = jnp.repeat(span_order, SPAN, total_repeat_length=total_rows) * SPAN + offsets % SPAN
    my_start = lax.axis_index("seq") * my_rows
    my_pos = lax.dynamic_slice_in_dim(all_pos, my_start, my_rows)
    my_q = q_rows.reshape(my_rows, heads_here, HEAD_DIM)
    my_k = k_rows.reshape(my_rows, heads_here, HEAD_DIM)
    my_v = v_rows.reshape(my_rows, heads_here, HEAD_DIM)
    my_g = g_rows.reshape(my_rows, heads_here, HEAD_DIM)

    def key_block_rows():
        return 512

    start_state = (
        jnp.full((heads_here, my_rows), -jnp.inf, jnp.float32),
        jnp.zeros((heads_here, my_rows), jnp.float32),
        jnp.zeros((heads_here, my_rows, HEAD_DIM), jnp.float32),
    )
    carry = start_state
    block_rows = key_block_rows()
    stacked, starts = split_blocks(
        (
            lax.all_gather(k_rows, "seq", axis=0, tiled=True),
            lax.all_gather(v_rows, "seq", axis=0, tiled=True),
        ),
        block_rows,
    )

    def forward_one_block(state, item):
        key_block, value_block, block_start = item
        key3 = key_block.reshape(block_rows, heads_here, HEAD_DIM)
        value3 = value_block.reshape(block_rows, heads_here, HEAD_DIM)
        positions = lax.dynamic_slice_in_dim(all_pos, block_start, block_rows)
        row_max, weight_sum, accum = state
        scores = masked_scores(my_q, key3, my_pos, positions, factor)
        new_max = jnp.maximum(row_max, jnp.max(scores, axis=2))
        safe_max = jnp.where(jnp.isfinite(new_max), new_max, 0.0)
        weights = jnp.exp(scores - safe_max[:, :, None])
        shrink = jnp.exp(row_max - safe_max)
        weight_sum = weight_sum * shrink + jnp.sum(weights, axis=2)
        accum = accum * shrink[:, :, None] + jnp.einsum(
            "hqk,khd->hqd", weights, value3.astype(jnp.float32)
        )
        return ((new_max, weight_sum, accum), None)

    carry, unused = lax.scan(forward_one_block, carry, stacked + (starts,))
    row_max, weight_sum, accum = carry
    lse_rows = (row_max + jnp.log(weight_sum)).T
    attended3 = jnp.transpose(accum / weight_sum[:, :, None], (1, 0, 2)).astype(jnp.bfloat16)
    delta_rows = jnp.sum(my_g.astype(jnp.float32) * attended3.astype(jnp.float32), axis=2)
    lse_all, delta_all = (
        lax.all_gather(lse_rows, "seq", axis=0, tiled=True),
        lax.all_gather(delta_rows, "seq", axis=0, tiled=True),
    )

    def pair_terms(
        q_block, g_block, lse_block, delta_block, q_pos, key_block, value_block, key_positions
    ):
        scores = masked_scores(q_block, key_block, q_pos, key_positions, factor)
        probs = jnp.exp(scores - lse_block.T[:, :, None])
        dprobs = jnp.einsum(
            "qhd,khd->hqk", g_block, value_block, preferred_element_type=jnp.float32
        )
        dscores = (probs * (dprobs - delta_block.T[:, :, None])).astype(jnp.bfloat16)
        return (probs.astype(jnp.bfloat16), dscores)

    def query_part(acc_q, key3, value3, positions):
        unused, dscores = pair_terms(
            my_q, my_g, lse_rows, delta_rows, my_pos, key3, value3, positions
        )
        return acc_q + jnp.einsum("hqk,khd->hqd", dscores, key3, preferred_element_type=jnp.float32)

    def key_part(acc_kv, q3, g3, block_start):
        positions = lax.dynamic_slice_in_dim(all_pos, block_start, my_rows)
        lse_block = lax.dynamic_slice_in_dim(lse_all, block_start, my_rows, 0)
        delta_block = lax.dynamic_slice_in_dim(delta_all, block_start, my_rows, 0)
        grad_k, grad_v = acc_kv
        probs_half, dscores = pair_terms(
            q3, g3, lse_block, delta_block, positions, my_k, my_v, my_pos
        )
        grad_k = grad_k + settle(
            jnp.einsum("hqk,qhd->khd", dscores, q3, preferred_element_type=jnp.float32) * factor
        )
        grad_v = grad_v + settle(
            jnp.einsum("hqk,qhd->khd", probs_half, g3, preferred_element_type=jnp.float32)
        )
        return (grad_k, grad_v)

    zeros_q = jnp.zeros((heads_here, my_rows, HEAD_DIM), jnp.float32)
    zeros_k = jnp.zeros((my_rows, heads_here, HEAD_DIM), jnp.float32)
    carry = zeros_q
    query_block_rows = key_block_rows()
    stacked, starts = split_blocks(
        (
            lax.all_gather(k_rows, "seq", axis=0, tiled=True),
            lax.all_gather(v_rows, "seq", axis=0, tiled=True),
        ),
        query_block_rows,
    )

    def query_one_block(state, item):
        key_block, value_block, block_start = item
        positions = lax.dynamic_slice_in_dim(all_pos, block_start, query_block_rows)
        key3 = key_block.reshape(query_block_rows, heads_here, HEAD_DIM)
        value3 = value_block.reshape(query_block_rows, heads_here, HEAD_DIM)
        return (query_part(state, key3, value3, positions), None)

    carry, unused = lax.scan(query_one_block, carry, stacked + (starts,))
    grad_q_acc = carry
    carry = (zeros_k, zeros_k)
    stacked, starts = split_blocks(
        (
            lax.all_gather(q_rows, "seq", axis=0, tiled=True),
            lax.all_gather(g_rows, "seq", axis=0, tiled=True),
        ),
        my_rows,
    )

    def key_one_block(state, item):
        query_block, cotangent_block, block_start = item
        q3 = query_block.reshape(my_rows, heads_here, HEAD_DIM)
        g3 = cotangent_block.reshape(my_rows, heads_here, HEAD_DIM)
        return (key_part(state, q3, g3, block_start), None)

    carry, unused = lax.scan(key_one_block, carry, stacked + (starts,))
    grad_k_acc, grad_v_acc = carry
    attended_rows = attended3.reshape(my_rows, heads_here * HEAD_DIM)
    grad_q_rows = (
        (jnp.transpose(grad_q_acc, (1, 0, 2)) * factor)
        .astype(jnp.bfloat16)
        .reshape(my_rows, heads_here * HEAD_DIM)
    )
    grad_k_rows = grad_k_acc.astype(jnp.bfloat16).reshape(my_rows, heads_here * HEAD_DIM)
    grad_v_rows = grad_v_acc.astype(jnp.bfloat16).reshape(my_rows, heads_here * HEAD_DIM)
    return (attended_rows, grad_q_rows, grad_k_rows, grad_v_rows)


F32 = jnp.float32
BF = jnp.bfloat16
NN = (((1,), (0,)), ((), ()))
NT = (((1,), (1,)), ((), ()))
LOG2E = 1.4426950408889634
FACTOR = HEAD_DIM**-0.5
BLOCK = 512


def dot(a, b, dims):
    return lax.dot_general(a, b, dims, preferred_element_type=F32)


def place_here():
    me = lax.axis_index("seq")
    side = lax.div(me, 2)
    owner = (me == 1) | (me == 2)
    return me, side, owner


def columns(half):
    return pl.ds(pl.multiple_of(half * HEAD_DIM, HEAD_DIM), HEAD_DIM)


def run_copies(copies):
    for one in copies:
        one.start()
    for one in copies:
        one.wait()


def owner_kernel(order_ref, own, s_l, s_r, s_c, o_own, o_l, o_r, o_c, q, k, v, g, kt, vt, s, dk, dv):
    me, side, held = place_here()
    rows = own.shape[0] // 4
    total = 4 * rows
    per = rows // SPAN
    far = 3 - 3 * side
    slots = ((me, own, o_own), (me - 1, s_l, o_l), (me + 1, s_r, o_r), (far, s_c, o_c))

    @pl.when(held)
    def _():
        places = [
            (src, dst, e, pl.ds(pl.multiple_of(order_ref[at * per + e] * SPAN, SPAN), SPAN))
            for at, src, dst in slots
            for e in range(per)
        ]
        part = lambda n, e: slice(n * rows + e * SPAN, n * rows + (e + 1) * SPAN)
        for src, _, e, where in places:
            for n, to in enumerate((q, k, v, g)):
                to[where, :] = src[part(n, e), :]
        key_at = lax.broadcasted_iota(jnp.int32, (BLOCK, BLOCK), 0)
        query_at = lax.broadcasted_iota(jnp.int32, (BLOCK, BLOCK), 1)
        for i in range(total // BLOCK):
            ri = slice(i * BLOCK, (i + 1) * BLOCK)
            kt[:, ri] = k[ri, :].T
            vt[:, ri] = v[ri, :].T
            qb = q[ri, :]
            top = None
            for j in range(i + 1):
                rj = slice(j * BLOCK, (j + 1) * BLOCK)
                sj = dot(k[rj, :], qb, NT) * (FACTOR * LOG2E)
                if j == i:
                    sj = jnp.where(key_at <= query_at, sj, -1e30)
                s[rj, :] = sj
                tj = jnp.max(sj, axis=0, keepdims=True)
                top = tj if top is None else jnp.maximum(top, tj)
            weight, acc = None, None
            for j in range(i + 1):
                rj = slice(j * BLOCK, (j + 1) * BLOCK)
                pj = jnp.exp2(s[rj, :] - top)
                s[rj, :] = pj
                lj = jnp.sum(pj, axis=0, keepdims=True)
                oj = dot(vt[:, rj], pj.astype(BF), NN)
                weight = lj if weight is None else weight + lj
                acc = oj if acc is None else acc + oj
            inverse = 1.0 / weight
            ob = (acc * inverse).astype(BF)
            gt = g[ri, :].T.astype(F32) * inverse
            gb = gt.astype(BF)
            delta = jnp.sum(gt * ob.astype(F32), axis=0, keepdims=True)
            acc = None
            for j in range(i + 1):
                rj = slice(j * BLOCK, (j + 1) * BLOCK)
                dp = dot(v[rj, :], gb, NN)
                pj = s[rj, :]
                ds = (pj * (dp - delta)).astype(BF)
                vj = dot(pj.astype(BF), gb, NT)
                kj = dot(ds, qb, NN)
                if j == i:
                    dv[rj, :] = vj
                    dk[rj, :] = kj
                else:
                    dv[rj, :] += vj
                    dk[rj, :] += kj
                qj = dot(kt[:, rj], ds, NN)
                acc = qj if acc is None else acc + qj
            q[ri, :] = (acc * FACTOR).astype(BF).T
            g[ri, :] = ob.T
        for _, dst, e, where in places:
            dst[part(0, e), :] = g[where, :]
            dst[part(1, e), :] = q[where, :]
            dst[part(2, e), :] = (dk[where, :] * FACTOR).astype(BF)
            dst[part(3, e), :] = dv[where, :].astype(BF)


def pack_kernel(q, k, v, g, hopl, hopr, rest, sem):
    sh = q.shape[0]
    _, side, owner = place_here()
    near_rest = jnp.where(owner, side, 1 - side)
    halves = ((hopl, 1 - near_rest), (hopr, 1 - near_rest), (rest, near_rest),)
    run_copies([
        pltpu.make_async_copy(src.at[:, columns(half)], dst.at[n * sh:(n + 1) * sh, :], sem.at[m, n])
        for m, (dst, half) in enumerate(halves)
        for n, src in enumerate((q, k, v, g))
    ])


def unpack_kernel(own, r_c, r_r, r_l, *refs):
    outs, sem = refs[:4], refs[4]
    sh = outs[0].shape[0]
    me, side, _ = place_here()
    for at, near, far in ((0, r_r, r_c), (1, own, r_r), (2, own, r_l), (3, r_l, r_c)):
        @pl.when(me == at)
        def _():
            run_copies([
                pltpu.make_async_copy(src.at[n * sh:(n + 1) * sh, :], dst.at[:, columns(half)], sem.at[m, n])
                for m, (src, half) in enumerate(((far, 1 - side), (near, side)))
                for n, dst in enumerate(outs)
            ])


def in_vmem(*shapes):
    return tuple(pltpu.VMEM(shape, dtype) for shape, dtype in shapes)


def kept(*arrays):
    return tuple(pltpu.with_memory_space_constraint(x, pltpu.VMEM) for x in arrays)


def owned_per_device(span_order, queries, keys, values, grad_out):
    rows = queries.shape[0]
    total = 4 * rows
    anywhere = pl.BlockSpec(memory_space=pl.ANY)
    vm = pl.BlockSpec(memory_space=pltpu.VMEM)
    sm = pl.BlockSpec(memory_space=pltpu.SMEM)
    stack = ((4 * rows, HEAD_DIM), BF)
    per_row = ((total, HEAD_DIM), BF)
    per_column = ((HEAD_DIM, total), BF)
    wide = ((total, HEAD_DIM), F32)
    hopl, hopr, rest = pl.pallas_call(
        pack_kernel,
        out_shape=in_vmem(*(stack,) * 3),
        in_specs=[anywhere] * 4,
        out_specs=(vm,) * 3,
        scratch_shapes=[pltpu.SemaphoreType.DMA((3, 4))],
        name="pack",
    )(queries, keys, values, grad_out)
    go = lambda x, pairs: lax.ppermute(x, "seq", pairs)
    g_l = go(hopr, [(0, 1), (1, 2)])
    g_r = go(hopl, [(3, 2), (2, 1)])
    g_c = go(rest, [(0, 2), (3, 1)])
    own, to_l, to_r, to_c = pl.pallas_call(
        owner_kernel,
        out_shape=in_vmem(*(stack,) * 4),
        in_specs=[sm] + [vm] * 4,
        out_specs=(vm,) * 4,
        scratch_shapes=[
            *in_vmem(per_row, per_row, per_row, per_row, per_column, per_column, ((total, BLOCK), F32), wide, wide)
        ],
        compiler_params=pltpu.CompilerParams(vmem_limit_bytes=32 << 20),
        name="owner",
    )(span_order, *kept(rest, g_l, g_r, g_c))
    r_r = go(to_l, [(1, 0), (2, 1)])
    r_l = go(to_r, [(1, 2), (2, 3)])
    r_c = go(to_c, [(1, 3), (2, 0)])
    return pl.pallas_call(
        unpack_kernel,
        out_shape=(jax.ShapeDtypeStruct(queries.shape, BF),) * 4,
        in_specs=[vm] * 4,
        out_specs=(anywhere,) * 4,
        scratch_shapes=[pltpu.SemaphoreType.DMA((2, 4))],
        name="unpack",
    )(*kept(own, r_c, r_r, r_l))


def solution(mesh):
    rows_columns = P(("groups", "seq"), ("head", "mp"))

    def run(span_order, queries, keys, values, grad_out):
        heads_here = queries.shape[1] // HEAD_DIM // (mesh.shape["head"] * mesh.shape["mp"])
        small = mesh.shape["seq"] == 4 and heads_here == 2
        return jax.shard_map(
            owned_per_device if small else gathered_per_device,
            mesh=mesh,
            in_specs=(P("groups"),) + (rows_columns,) * 4,
            out_specs=(rows_columns,) * 4,
            check_vma=False,
        )(span_order, queries, keys, values, grad_out)

    return run
```

```python
import jax
import jax.numpy as jnp
from jax import lax
from jax.experimental import pallas as pl
from jax.experimental.pallas import tpu as pltpu
from jax.sharding import PartitionSpec as P

HEAD_DIM = 128
SPAN = 128


def settle(values_in):
    return lax.optimization_barrier(values_in.astype(jnp.bfloat16)).astype(jnp.float32)


def masked_scores(query_block, key_block, query_pos, key_positions, factor):
    raw = (
        jnp.einsum("qhd,khd->hqk", query_block, key_block, preferred_element_type=jnp.float32)
        * factor
    )
    return jnp.where(key_positions[None, None, :] <= query_pos[None, :, None], raw, -jnp.inf)


def split_blocks(arrays, block_rows):
    count_blocks = arrays[0].shape[0] // block_rows
    stacked = tuple(
        (member.reshape((count_blocks, block_rows) + member.shape[1:]) for member in arrays)
    )
    starts = jnp.arange(count_blocks, dtype=jnp.int32) * block_rows
    return (stacked, starts)


def gathered_per_device(span_order, queries, keys, values, grad_out):
    q_rows, k_rows, v_rows, g_rows = (queries, keys, values, grad_out)
    my_rows = q_rows.shape[0]
    heads_here = q_rows.shape[1] // HEAD_DIM
    factor = HEAD_DIM ** (-0.5)
    total_rows = span_order.shape[0] * SPAN
    offsets = jnp.arange(total_rows, dtype=jnp.int32)
    all_pos = jnp.repeat(span_order, SPAN, total_repeat_length=total_rows) * SPAN + offsets % SPAN
    my_start = lax.axis_index("seq") * my_rows
    my_pos = lax.dynamic_slice_in_dim(all_pos, my_start, my_rows)
    my_q = q_rows.reshape(my_rows, heads_here, HEAD_DIM)
    my_k = k_rows.reshape(my_rows, heads_here, HEAD_DIM)
    my_v = v_rows.reshape(my_rows, heads_here, HEAD_DIM)
    my_g = g_rows.reshape(my_rows, heads_here, HEAD_DIM)

    def key_block_rows():
        return 512

    start_state = (
        jnp.full((heads_here, my_rows), -jnp.inf, jnp.float32),
        jnp.zeros((heads_here, my_rows), jnp.float32),
        jnp.zeros((heads_here, my_rows, HEAD_DIM), jnp.float32),
    )
    carry = start_state
    block_rows = key_block_rows()
    stacked, starts = split_blocks(
        (
            lax.all_gather(k_rows, "seq", axis=0, tiled=True),
            lax.all_gather(v_rows, "seq", axis=0, tiled=True),
        ),
        block_rows,
    )

    def forward_one_block(state, item):
        key_block, value_block, block_start = item
        key3 = key_block.reshape(block_rows, heads_here, HEAD_DIM)
        value3 = value_block.reshape(block_rows, heads_here, HEAD_DIM)
        positions = lax.dynamic_slice_in_dim(all_pos, block_start, block_rows)
        row_max, weight_sum, accum = state
        scores = masked_scores(my_q, key3, my_pos, positions, factor)
        new_max = jnp.maximum(row_max, jnp.max(scores, axis=2))
        safe_max = jnp.where(jnp.isfinite(new_max), new_max, 0.0)
        weights = jnp.exp(scores - safe_max[:, :, None])
        shrink = jnp.exp(row_max - safe_max)
        weight_sum = weight_sum * shrink + jnp.sum(weights, axis=2)
        accum = accum * shrink[:, :, None] + jnp.einsum(
            "hqk,khd->hqd", weights, value3.astype(jnp.float32)
        )
        return ((new_max, weight_sum, accum), None)

    carry, unused = lax.scan(forward_one_block, carry, stacked + (starts,))
    row_max, weight_sum, accum = carry
    lse_rows = (row_max + jnp.log(weight_sum)).T
    attended3 = jnp.transpose(accum / weight_sum[:, :, None], (1, 0, 2)).astype(jnp.bfloat16)
    delta_rows = jnp.sum(my_g.astype(jnp.float32) * attended3.astype(jnp.float32), axis=2)
    lse_all, delta_all = (
        lax.all_gather(lse_rows, "seq", axis=0, tiled=True),
        lax.all_gather(delta_rows, "seq", axis=0, tiled=True),
    )

    def pair_terms(
        q_block, g_block, lse_block, delta_block, q_pos, key_block, value_block, key_positions
    ):
        scores = masked_scores(q_block, key_block, q_pos, key_positions, factor)
        probs = jnp.exp(scores - lse_block.T[:, :, None])
        dprobs = jnp.einsum(
            "qhd,khd->hqk", g_block, value_block, preferred_element_type=jnp.float32
        )
        dscores = (probs * (dprobs - delta_block.T[:, :, None])).astype(jnp.bfloat16)
        return (probs.astype(jnp.bfloat16), dscores)

    def query_part(acc_q, key3, value3, positions):
        unused, dscores = pair_terms(
            my_q, my_g, lse_rows, delta_rows, my_pos, key3, value3, positions
        )
        return acc_q + jnp.einsum("hqk,khd->hqd", dscores, key3, preferred_element_type=jnp.float32)

    def key_part(acc_kv, q3, g3, block_start):
        positions = lax.dynamic_slice_in_dim(all_pos, block_start, my_rows)
        lse_block = lax.dynamic_slice_in_dim(lse_all, block_start, my_rows, 0)
        delta_block = lax.dynamic_slice_in_dim(delta_all, block_start, my_rows, 0)
        grad_k, grad_v = acc_kv
        probs_half, dscores = pair_terms(
            q3, g3, lse_block, delta_block, positions, my_k, my_v, my_pos
        )
        grad_k = grad_k + settle(
            jnp.einsum("hqk,qhd->khd", dscores, q3, preferred_element_type=jnp.float32) * factor
        )
        grad_v = grad_v + settle(
            jnp.einsum("hqk,qhd->khd", probs_half, g3, preferred_element_type=jnp.float32)
        )
        return (grad_k, grad_v)

    zeros_q = jnp.zeros((heads_here, my_rows, HEAD_DIM), jnp.float32)
    zeros_k = jnp.zeros((my_rows, heads_here, HEAD_DIM), jnp.float32)
    carry = zeros_q
    query_block_rows = key_block_rows()
    stacked, starts = split_blocks(
        (
            lax.all_gather(k_rows, "seq", axis=0, tiled=True),
            lax.all_gather(v_rows, "seq", axis=0, tiled=True),
        ),
        query_block_rows,
    )

    def query_one_block(state, item):
        key_block, value_block, block_start = item
        positions = lax.dynamic_slice_in_dim(all_pos, block_start, query_block_rows)
        key3 = key_block.reshape(query_block_rows, heads_here, HEAD_DIM)
        value3 = value_block.reshape(query_block_rows, heads_here, HEAD_DIM)
        return (query_part(state, key3, value3, positions), None)

    carry, unused = lax.scan(query_one_block, carry, stacked + (starts,))
    grad_q_acc = carry
    carry = (zeros_k, zeros_k)
    stacked, starts = split_blocks(
        (
            lax.all_gather(q_rows, "seq", axis=0, tiled=True),
            lax.all_gather(g_rows, "seq", axis=0, tiled=True),
        ),
        my_rows,
    )

    def key_one_block(state, item):
        query_block, cotangent_block, block_start = item
        q3 = query_block.reshape(my_rows, heads_here, HEAD_DIM)
        g3 = cotangent_block.reshape(my_rows, heads_here, HEAD_DIM)
        return (key_part(state, q3, g3, block_start), None)

    carry, unused = lax.scan(key_one_block, carry, stacked + (starts,))
    grad_k_acc, grad_v_acc = carry
    attended_rows = attended3.reshape(my_rows, heads_here * HEAD_DIM)
    grad_q_rows = (
        (jnp.transpose(grad_q_acc, (1, 0, 2)) * factor)
        .astype(jnp.bfloat16)
        .reshape(my_rows, heads_here * HEAD_DIM)
    )
    grad_k_rows = grad_k_acc.astype(jnp.bfloat16).reshape(my_rows, heads_here * HEAD_DIM)
    grad_v_rows = grad_v_acc.astype(jnp.bfloat16).reshape(my_rows, heads_here * HEAD_DIM)
    return (attended_rows, grad_q_rows, grad_k_rows, grad_v_rows)


F32 = jnp.float32
BF = jnp.bfloat16
NN = (((1,), (0,)), ((), ()))
NT = (((1,), (1,)), ((), ()))
LOG2E = 1.4426950408889634
FACTOR = HEAD_DIM**-0.5
BLOCK = 512
HALF = 256


def dot(a, b, dims):
    return lax.dot_general(a, b, dims, preferred_element_type=F32)


def place_here():
    me = lax.axis_index("seq")
    side = lax.div(me, 2)
    owner = (me == 1) | (me == 2)
    return me, side, owner


def columns(half):
    return pl.ds(pl.multiple_of(half * HEAD_DIM, HEAD_DIM), HEAD_DIM)


def run_copies(copies):
    for one in copies:
        one.start()
    for one in copies:
        one.wait()


def owner_kernel(order_ref, own, s_l, s_r, s_c, o_own, o_c, o_a, o_b, q, k, v, g, kt, vt, s, dk, dv):
    me, side, held = place_here()
    rows = own.shape[0] // 4
    total = 4 * rows
    per = rows // SPAN
    near_at, far_at = 3 * side, 3 - 3 * side
    slots_in = ((me, own), (me - 1, s_l), (me + 1, s_r), (far_at, s_c))
    slots_out = ((me, o_own), (far_at, o_c), (near_at, o_a), (3 - me, o_b))

    @pl.when(held)
    def _():
        places = lambda slots: [
            (ref, e, pl.ds(pl.multiple_of(order_ref[at * per + e] * SPAN, SPAN), SPAN))
            for at, ref in slots
            for e in range(per)
        ]
        part = lambda n, e: slice(n * rows + e * SPAN, n * rows + (e + 1) * SPAN)
        for src, e, where in places(slots_in):
            for n, to in enumerate((q, k, v, g)):
                to[where, :] = src[part(n, e), :]
        key_at = lax.broadcasted_iota(jnp.int32, (HALF, HALF), 0)
        query_at = lax.broadcasted_iota(jnp.int32, (HALF, HALF), 1)
        seen = key_at <= query_at
        tail = lambda whole, part: jnp.concatenate([whole[:, :HALF], part(whole[:, HALF:])], axis=1)
        for i in range(total // BLOCK):
            lo = slice(i * BLOCK, i * BLOCK + HALF)
            hi = slice(i * BLOCK + HALF, (i + 1) * BLOCK)
            ri = slice(i * BLOCK, (i + 1) * BLOCK)
            olds = [slice(j * BLOCK, (j + 1) * BLOCK) for j in range(i)] + [lo]
            kt[:, ri] = k[ri, :].T
            vt[:, ri] = v[ri, :].T
            qb = q[ri, :]
            qh = q[hi, :]
            top = None
            for rj in olds:
                sj = dot(k[rj, :], qb, NT) * (FACTOR * LOG2E)
                if rj is lo:
                    sj = jnp.concatenate([jnp.where(seen, sj[:, :HALF], -1e30), sj[:, HALF:]], axis=1)
                s[rj, ri] = sj
                tj = jnp.max(sj, axis=0, keepdims=True)
                top = tj if top is None else jnp.maximum(top, tj)
            sh = jnp.where(seen, dot(k[hi, :], qh, NT) * (FACTOR * LOG2E), -1e30)
            s[hi, hi] = sh
            top = tail(top, lambda x: jnp.maximum(x, jnp.max(sh, axis=0, keepdims=True)))
            weight, acc = None, None
            for rj in olds:
                pj = jnp.exp2(s[rj, ri] - top)
                s[rj, ri] = pj
                lj = jnp.sum(pj, axis=0, keepdims=True)
                oj = dot(vt[:, rj], pj.astype(BF), NN)
                weight = lj if weight is None else weight + lj
                acc = oj if acc is None else acc + oj
            ph = jnp.exp2(s[hi, hi] - top[:, HALF:])
            s[hi, hi] = ph
            weight = tail(weight, lambda x: x + jnp.sum(ph, axis=0, keepdims=True))
            acc = tail(acc, lambda x: x + dot(vt[:, hi], ph.astype(BF), NN))
            inverse = 1.0 / weight
            ob = (acc * inverse).astype(BF)
            gt = g[ri, :].T.astype(F32) * inverse
            gb = gt.astype(BF)
            delta = jnp.sum(gt * ob.astype(F32), axis=0, keepdims=True)
            acc = None
            for rj in olds:
                dp = dot(v[rj, :], gb, NN)
                pj = s[rj, ri]
                ds = (pj * (dp - delta)).astype(BF)
                vj = dot(pj.astype(BF), gb, NT)
                kj = dot(ds, qb, NN)
                if rj is lo:
                    dv[rj, :] = vj
                    dk[rj, :] = kj
                else:
                    dv[rj, :] += vj
                    dk[rj, :] += kj
                qj = dot(kt[:, rj], ds, NN)
                acc = qj if acc is None else acc + qj
            dp = dot(v[hi, :], gb[:, HALF:], NN)
            ph = s[hi, hi]
            ds = (ph * (dp - delta[:, HALF:])).astype(BF)
            dv[hi, :] = dot(ph.astype(BF), gb[:, HALF:], NT)
            dk[hi, :] = dot(ds, qh, NN)
            acc = tail(acc, lambda x: x + dot(kt[:, hi], ds, NN))
            q[ri, :] = (acc * FACTOR).astype(BF).T
            g[ri, :] = ob.T
        for dst, e, where in places(slots_out):
            dst[part(0, e), :] = g[where, :]
            dst[part(1, e), :] = q[where, :]
            dst[part(2, e), :] = (dk[where, :] * FACTOR).astype(BF)
            dst[part(3, e), :] = dv[where, :].astype(BF)


def pack_kernel(order, q, k, v, g, hopl, hopr, rest, order_out, sem, order_sem):
    sh = q.shape[0]
    _, side, owner = place_here()
    near_rest = jnp.where(owner, side, 1 - side)
    halves = ((hopl, 1 - near_rest), (hopr, 1 - near_rest), (rest, near_rest),)
    run_copies([
        pltpu.make_async_copy(src.at[:, columns(half)], dst.at[n * sh:(n + 1) * sh, :], sem.at[m, n])
        for m, (dst, half) in enumerate(halves)
        for n, src in enumerate((q, k, v, g))
    ] + [pltpu.make_async_copy(order, order_out, order_sem)])


def unpack_kernel(own, r_c, r_a, r_b, *refs):
    outs, sem = refs[:4], refs[4]
    sh = outs[0].shape[0]
    me, side, _ = place_here()
    for at, near, far in ((0, r_a, r_c), (1, own, r_b), (2, own, r_b), (3, r_a, r_c)):
        @pl.when(me == at)
        def _():
            run_copies([
                pltpu.make_async_copy(src.at[n * sh:(n + 1) * sh, :], dst.at[:, columns(half)], sem.at[m, n])
                for m, (src, half) in enumerate(((far, 1 - side), (near, side)))
                for n, dst in enumerate(outs)
            ])


def in_vmem(*shapes):
    return tuple(pltpu.VMEM(shape, dtype) for shape, dtype in shapes)


def kept(*arrays):
    return tuple(pltpu.with_memory_space_constraint(x, pltpu.VMEM) for x in arrays)


def owned_per_device(span_order, queries, keys, values, grad_out):
    rows = queries.shape[0]
    total = 4 * rows
    anywhere = pl.BlockSpec(memory_space=pl.ANY)
    vm = pl.BlockSpec(memory_space=pltpu.VMEM)
    sm = pl.BlockSpec(memory_space=pltpu.SMEM)
    stack = ((4 * rows, HEAD_DIM), BF)
    per_row = ((total, HEAD_DIM), BF)
    per_column = ((HEAD_DIM, total), BF)
    wide = ((total, HEAD_DIM), F32)
    hopl, hopr, rest, order = pl.pallas_call(
        pack_kernel,
        out_shape=in_vmem(*(stack,) * 3) + (pltpu.SMEM(span_order.shape, span_order.dtype),),
        in_specs=[anywhere] * 5,
        out_specs=(vm,) * 3 + (sm,),
        scratch_shapes=[pltpu.SemaphoreType.DMA((3, 4)), pltpu.SemaphoreType.DMA],
        name="pack",
    )(span_order, queries, keys, values, grad_out)
    go = lambda x, pairs: lax.ppermute(x, "seq", pairs)
    g_l = go(hopr, [(0, 1), (1, 2)])
    g_r = go(hopl, [(3, 2), (2, 1)])
    g_c = go(rest, [(0, 2), (3, 1)])
    own, to_c, to_a, to_b = pl.pallas_call(
        owner_kernel,
        out_shape=in_vmem(*(stack,) * 4),
        in_specs=[sm] + [vm] * 4,
        out_specs=(vm,) * 4,
        scratch_shapes=[
            *in_vmem(per_row, per_row, per_row, per_row, per_column, per_column, ((total, total), F32), wide, wide)
        ],
        compiler_params=pltpu.CompilerParams(vmem_limit_bytes=32 << 20),
        name="owner",
    )(order, *kept(rest, g_l, g_r, g_c))
    r_a = go(to_a, [(1, 0), (2, 3)])
    r_b = go(to_b, [(1, 2), (2, 1)])
    r_c = go(to_c, [(1, 3), (2, 0)])
    return pl.pallas_call(
        unpack_kernel,
        out_shape=(jax.ShapeDtypeStruct(queries.shape, BF),) * 4,
        in_specs=[vm] * 4,
        out_specs=(anywhere,) * 4,
        scratch_shapes=[pltpu.SemaphoreType.DMA((2, 4))],
        name="unpack",
    )(*kept(own, r_c, r_a, r_b))


def solution(mesh):
    rows_columns = P(("groups", "seq"), ("head", "mp"))

    def run(span_order, queries, keys, values, grad_out):
        heads_here = queries.shape[1] // HEAD_DIM // (mesh.shape["head"] * mesh.shape["mp"])
        small = mesh.shape["seq"] == 4 and heads_here == 2
        return jax.shard_map(
            owned_per_device if small else gathered_per_device,
            mesh=mesh,
            in_specs=(P("groups"),) + (rows_columns,) * 4,
            out_specs=(rows_columns,) * 4,
            check_vma=False,
        )(span_order, queries, keys, values, grad_out)

    return run
```

```python
import functools

import jax
import jax.numpy as jnp
from jax import lax
from jax.experimental import pallas as pl
from jax.experimental.pallas import tpu as pltpu
from jax.sharding import PartitionSpec as P

HEAD_DIM = 128
SPAN = 128


def settle(values_in):
    return lax.optimization_barrier(values_in.astype(jnp.bfloat16)).astype(jnp.float32)


def masked_scores(query_block, key_block, query_pos, key_positions, factor):
    raw = (
        jnp.einsum("qhd,khd->hqk", query_block, key_block, preferred_element_type=jnp.float32)
        * factor
    )
    return jnp.where(key_positions[None, None, :] <= query_pos[None, :, None], raw, -jnp.inf)


def split_blocks(arrays, block_rows):
    count_blocks = arrays[0].shape[0] // block_rows
    stacked = tuple(
        (member.reshape((count_blocks, block_rows) + member.shape[1:]) for member in arrays)
    )
    starts = jnp.arange(count_blocks, dtype=jnp.int32) * block_rows
    return (stacked, starts)


def gathered_per_device(span_order, queries, keys, values, grad_out):
    q_rows, k_rows, v_rows, g_rows = (queries, keys, values, grad_out)
    my_rows = q_rows.shape[0]
    heads_here = q_rows.shape[1] // HEAD_DIM
    factor = HEAD_DIM ** (-0.5)
    total_rows = span_order.shape[0] * SPAN
    offsets = jnp.arange(total_rows, dtype=jnp.int32)
    all_pos = jnp.repeat(span_order, SPAN, total_repeat_length=total_rows) * SPAN + offsets % SPAN
    my_start = lax.axis_index("seq") * my_rows
    my_pos = lax.dynamic_slice_in_dim(all_pos, my_start, my_rows)
    my_q = q_rows.reshape(my_rows, heads_here, HEAD_DIM)
    my_k = k_rows.reshape(my_rows, heads_here, HEAD_DIM)
    my_v = v_rows.reshape(my_rows, heads_here, HEAD_DIM)
    my_g = g_rows.reshape(my_rows, heads_here, HEAD_DIM)

    def key_block_rows():
        return 512

    start_state = (
        jnp.full((heads_here, my_rows), -jnp.inf, jnp.float32),
        jnp.zeros((heads_here, my_rows), jnp.float32),
        jnp.zeros((heads_here, my_rows, HEAD_DIM), jnp.float32),
    )
    carry = start_state
    block_rows = key_block_rows()
    stacked, starts = split_blocks(
        (
            lax.all_gather(k_rows, "seq", axis=0, tiled=True),
            lax.all_gather(v_rows, "seq", axis=0, tiled=True),
        ),
        block_rows,
    )

    def forward_one_block(state, item):
        key_block, value_block, block_start = item
        key3 = key_block.reshape(block_rows, heads_here, HEAD_DIM)
        value3 = value_block.reshape(block_rows, heads_here, HEAD_DIM)
        positions = lax.dynamic_slice_in_dim(all_pos, block_start, block_rows)
        row_max, weight_sum, accum = state
        scores = masked_scores(my_q, key3, my_pos, positions, factor)
        new_max = jnp.maximum(row_max, jnp.max(scores, axis=2))
        safe_max = jnp.where(jnp.isfinite(new_max), new_max, 0.0)
        weights = jnp.exp(scores - safe_max[:, :, None])
        shrink = jnp.exp(row_max - safe_max)
        weight_sum = weight_sum * shrink + jnp.sum(weights, axis=2)
        accum = accum * shrink[:, :, None] + jnp.einsum(
            "hqk,khd->hqd", weights, value3.astype(jnp.float32)
        )
        return ((new_max, weight_sum, accum), None)

    carry, unused = lax.scan(forward_one_block, carry, stacked + (starts,))
    row_max, weight_sum, accum = carry
    lse_rows = (row_max + jnp.log(weight_sum)).T
    attended3 = jnp.transpose(accum / weight_sum[:, :, None], (1, 0, 2)).astype(jnp.bfloat16)
    delta_rows = jnp.sum(my_g.astype(jnp.float32) * attended3.astype(jnp.float32), axis=2)
    lse_all, delta_all = (
        lax.all_gather(lse_rows, "seq", axis=0, tiled=True),
        lax.all_gather(delta_rows, "seq", axis=0, tiled=True),
    )

    def pair_terms(
        q_block, g_block, lse_block, delta_block, q_pos, key_block, value_block, key_positions
    ):
        scores = masked_scores(q_block, key_block, q_pos, key_positions, factor)
        probs = jnp.exp(scores - lse_block.T[:, :, None])
        dprobs = jnp.einsum(
            "qhd,khd->hqk", g_block, value_block, preferred_element_type=jnp.float32
        )
        dscores = (probs * (dprobs - delta_block.T[:, :, None])).astype(jnp.bfloat16)
        return (probs.astype(jnp.bfloat16), dscores)

    def query_part(acc_q, key3, value3, positions):
        unused, dscores = pair_terms(
            my_q, my_g, lse_rows, delta_rows, my_pos, key3, value3, positions
        )
        return acc_q + jnp.einsum("hqk,khd->hqd", dscores, key3, preferred_element_type=jnp.float32)

    def key_part(acc_kv, q3, g3, block_start):
        positions = lax.dynamic_slice_in_dim(all_pos, block_start, my_rows)
        lse_block = lax.dynamic_slice_in_dim(lse_all, block_start, my_rows, 0)
        delta_block = lax.dynamic_slice_in_dim(delta_all, block_start, my_rows, 0)
        grad_k, grad_v = acc_kv
        probs_half, dscores = pair_terms(
            q3, g3, lse_block, delta_block, positions, my_k, my_v, my_pos
        )
        grad_k = grad_k + settle(
            jnp.einsum("hqk,qhd->khd", dscores, q3, preferred_element_type=jnp.float32) * factor
        )
        grad_v = grad_v + settle(
            jnp.einsum("hqk,qhd->khd", probs_half, g3, preferred_element_type=jnp.float32)
        )
        return (grad_k, grad_v)

    zeros_q = jnp.zeros((heads_here, my_rows, HEAD_DIM), jnp.float32)
    zeros_k = jnp.zeros((my_rows, heads_here, HEAD_DIM), jnp.float32)
    carry = zeros_q
    query_block_rows = key_block_rows()
    stacked, starts = split_blocks(
        (
            lax.all_gather(k_rows, "seq", axis=0, tiled=True),
            lax.all_gather(v_rows, "seq", axis=0, tiled=True),
        ),
        query_block_rows,
    )

    def query_one_block(state, item):
        key_block, value_block, block_start = item
        positions = lax.dynamic_slice_in_dim(all_pos, block_start, query_block_rows)
        key3 = key_block.reshape(query_block_rows, heads_here, HEAD_DIM)
        value3 = value_block.reshape(query_block_rows, heads_here, HEAD_DIM)
        return (query_part(state, key3, value3, positions), None)

    carry, unused = lax.scan(query_one_block, carry, stacked + (starts,))
    grad_q_acc = carry
    carry = (zeros_k, zeros_k)
    stacked, starts = split_blocks(
        (
            lax.all_gather(q_rows, "seq", axis=0, tiled=True),
            lax.all_gather(g_rows, "seq", axis=0, tiled=True),
        ),
        my_rows,
    )

    def key_one_block(state, item):
        query_block, cotangent_block, block_start = item
        q3 = query_block.reshape(my_rows, heads_here, HEAD_DIM)
        g3 = cotangent_block.reshape(my_rows, heads_here, HEAD_DIM)
        return (key_part(state, q3, g3, block_start), None)

    carry, unused = lax.scan(key_one_block, carry, stacked + (starts,))
    grad_k_acc, grad_v_acc = carry
    attended_rows = attended3.reshape(my_rows, heads_here * HEAD_DIM)
    grad_q_rows = (
        (jnp.transpose(grad_q_acc, (1, 0, 2)) * factor)
        .astype(jnp.bfloat16)
        .reshape(my_rows, heads_here * HEAD_DIM)
    )
    grad_k_rows = grad_k_acc.astype(jnp.bfloat16).reshape(my_rows, heads_here * HEAD_DIM)
    grad_v_rows = grad_v_acc.astype(jnp.bfloat16).reshape(my_rows, heads_here * HEAD_DIM)
    return (attended_rows, grad_q_rows, grad_k_rows, grad_v_rows)


F32 = jnp.float32
BF = jnp.bfloat16
NN = (((1,), (0,)), ((), ()))
NT = (((1,), (1,)), ((), ()))
LOG2E = 1.4426950408889634
FACTOR = HEAD_DIM**-0.5
BLOCK = 512
HALF = 256


def dot(a, b, dims):
    return lax.dot_general(a, b, dims, preferred_element_type=F32)


def place_here():
    me = lax.axis_index("seq")
    side = lax.div(me, 2)
    owner = (me == 1) | (me == 2)
    return me, side, owner


def columns(half):
    return pl.ds(pl.multiple_of(half * HEAD_DIM, HEAD_DIM), HEAD_DIM)


def run_copies(copies):
    for one in copies:
        one.start()
    for one in copies:
        one.wait()


def owner_kernel(order_ref, turn, own, s_c1, s_a1, s_b1, s_a0, s_b0, s_c0, o_own, o_a, o_c, o_b, q, k, v, g, kt, vt, s, dk, dv):
    me, side, held = place_here()
    rows = own.shape[0] // 4
    total = 4 * rows
    per = rows // SPAN
    near_at, far_at = 3 * side, 3 - 3 * side
    slots_out = ((me, o_own), (near_at, o_a), (far_at, o_c), (3 - me, o_b))

    @pl.when(held)
    def _():
        places = lambda slots: [
            (ref, e, pl.ds(pl.multiple_of(order_ref[at * per + e] * SPAN, SPAN), SPAN))
            for at, ref in slots
            for e in range(per)
        ]
        part = lambda n, e: slice(n * rows + e * SPAN, n * rows + (e + 1) * SPAN)
        def collect(slots):
            for src, e, where in places(slots):
                for n, to in enumerate((q, k, v, g)):
                    to[where, :] = src[part(n, e), :]

        for core, arrived in enumerate((
            ((me, own), (far_at, s_c0), (near_at, s_a0), (3 - me, s_b0)),
            ((me, own), (far_at, s_c1), (near_at, s_a1), (3 - me, s_b1)),
        )):
            pl.when(lax.axis_index("mp") == core)(functools.partial(collect, arrived))
        key_at = lax.broadcasted_iota(jnp.int32, (HALF, HALF), 0)
        query_at = lax.broadcasted_iota(jnp.int32, (HALF, HALF), 1)
        seen = key_at <= query_at
        tail = lambda whole, part: jnp.concatenate([whole[:, :HALF], part(whole[:, HALF:])], axis=1)
        for i in range(total // BLOCK):
            lo = slice(i * BLOCK, i * BLOCK + HALF)
            hi = slice(i * BLOCK + HALF, (i + 1) * BLOCK)
            ri = slice(i * BLOCK, (i + 1) * BLOCK)
            olds = [slice(j * BLOCK, (j + 1) * BLOCK) for j in range(i)] + [lo]
            kt[:, ri] = k[ri, :].T
            vt[:, ri] = v[ri, :].T
            qb = q[ri, :]
            qh = q[hi, :]
            top = None
            for rj in olds:
                sj = dot(k[rj, :], qb, NT) * (FACTOR * LOG2E)
                if rj is lo:
                    sj = jnp.concatenate([jnp.where(seen, sj[:, :HALF], -1e30), sj[:, HALF:]], axis=1)
                s[rj, ri] = sj
                tj = jnp.max(sj, axis=0, keepdims=True)
                top = tj if top is None else jnp.maximum(top, tj)
            sh = jnp.where(seen, dot(k[hi, :], qh, NT) * (FACTOR * LOG2E), -1e30)
            s[hi, hi] = sh
            top = tail(top, lambda x: jnp.maximum(x, jnp.max(sh, axis=0, keepdims=True)))
            weight, acc = None, None
            for rj in olds:
                pj = jnp.exp2(s[rj, ri] - top)
                s[rj, ri] = pj
                lj = jnp.sum(pj, axis=0, keepdims=True)
                oj = dot(vt[:, rj], pj.astype(BF), NN)
                weight = lj if weight is None else weight + lj
                acc = oj if acc is None else acc + oj
            ph = jnp.exp2(s[hi, hi] - top[:, HALF:])
            s[hi, hi] = ph
            weight = tail(weight, lambda x: x + jnp.sum(ph, axis=0, keepdims=True))
            acc = tail(acc, lambda x: x + dot(vt[:, hi], ph.astype(BF), NN))
            inverse = 1.0 / weight
            ob = (acc * inverse).astype(BF)
            gt = g[ri, :].T.astype(F32) * inverse
            gb = gt.astype(BF)
            delta = jnp.sum(gt * ob.astype(F32), axis=0, keepdims=True)
            acc = None
            for rj in olds:
                dp = dot(v[rj, :], gb, NN)
                pj = s[rj, ri]
                ds = (pj * (dp - delta)).astype(BF)
                vj = dot(pj.astype(BF), gb, NT)
                kj = dot(ds, qb, NN)
                if rj is lo:
                    dv[rj, :] = vj
                    dk[rj, :] = kj
                else:
                    dv[rj, :] += vj
                    dk[rj, :] += kj
                qj = dot(kt[:, rj], ds, NN)
                acc = qj if acc is None else acc + qj
            dp = dot(v[hi, :], gb[:, HALF:], NN)
            ph = s[hi, hi]
            ds = (ph * (dp - delta[:, HALF:])).astype(BF)
            dv[hi, :] = dot(ph.astype(BF), gb[:, HALF:], NT)
            dk[hi, :] = dot(ds, qh, NN)
            acc = tail(acc, lambda x: x + dot(kt[:, hi], ds, NN))
            q[ri, :] = (acc * FACTOR).astype(BF).T
            g[ri, :] = ob.T
        for dst, e, where in places(slots_out):
            dst[part(0, e), :] = g[where, :]
            dst[part(1, e), :] = q[where, :]
            dst[part(2, e), :] = (dk[where, :] * FACTOR).astype(BF)
            dst[part(3, e), :] = dv[where, :].astype(BF)


def pack_kernel(order, q, k, v, g, rest1, hopl1, hopr1, hopl0, hopr0, rest0, mine, turn, order_out, sem, order_sem):
    sh = q.shape[0]
    _, side, owner = place_here()
    rest_half = jnp.where(owner, side, 1 - side)
    turn[...] = jnp.zeros_like(turn)
    for core, hopl, hopr, rest in ((0, hopl0, hopr0, rest0), (1, hopl1, hopr1, rest1)):
        @pl.when(lax.axis_index("mp") == core)
        def _():
            halves = ((rest, 1 - side), (hopl, 1 - rest_half), (hopr, 1 - rest_half), (mine, side))
            run_copies([
                pltpu.make_async_copy(src.at[:, columns(half)], dst.at[n * sh:(n + 1) * sh, :], sem.at[m, n])
                for m, (dst, half) in enumerate(halves)
                for n, src in enumerate((q, k, v, g))
            ] + [pltpu.make_async_copy(order, order_out, order_sem)])


def unpack_kernel(own, r_a, r_c, r_b, *refs):
    outs, sem = refs[:4], refs[4]
    sh = outs[0].shape[0]
    me, side, _ = place_here()
    for at, near, far in ((0, r_a, r_c), (1, own, r_b), (2, own, r_b), (3, r_a, r_c)):
        @pl.when(me == at)
        def _():
            run_copies([
                pltpu.make_async_copy(src.at[n * sh:(n + 1) * sh, :], dst.at[:, columns(half)], sem.at[m, n])
                for m, (src, half) in enumerate(((far, 1 - side), (near, side)))
                for n, dst in enumerate(outs)
            ])


def in_vmem(*shapes):
    return tuple(pltpu.VMEM(shape, dtype) for shape, dtype in shapes)


def kept(*arrays):
    return tuple(pltpu.with_memory_space_constraint(x, pltpu.VMEM) for x in arrays)


def owned_per_device(span_order, queries, keys, values, grad_out):
    rows = queries.shape[0]
    total = 4 * rows
    anywhere = pl.BlockSpec(memory_space=pl.ANY)
    vm = pl.BlockSpec(memory_space=pltpu.VMEM)
    sm = pl.BlockSpec(memory_space=pltpu.SMEM)
    stack = ((4 * rows, HEAD_DIM), BF)
    per_row = ((total, HEAD_DIM), BF)
    per_column = ((HEAD_DIM, total), BF)
    wide = ((total, HEAD_DIM), F32)
    rest1, hopl1, hopr1, hopl0, hopr0, rest0, mine, turn, order = pl.pallas_call(
        pack_kernel,
        out_shape=in_vmem(*(stack,) * 7, ((16, HEAD_DIM), BF)) + (pltpu.SMEM(span_order.shape, span_order.dtype),),
        in_specs=[anywhere] * 5,
        out_specs=(vm,) * 8 + (sm,),
        scratch_shapes=[pltpu.SemaphoreType.DMA((4, 4)), pltpu.SemaphoreType.DMA],
        name="pack",
    )(span_order, queries, keys, values, grad_out)
    go = lambda x, pairs: lax.ppermute(x, "seq", pairs)

    def go_core(x, pairs, core):
        return lax.ppermute(x, ("seq", "mp"), [(2 * a + core, 2 * b + core) for a, b in pairs])

    g_c1 = go_core(rest1, [(0, 2), (3, 1)], 1)
    g_a1 = go_core(hopl1, [(0, 1), (3, 2)], 1)
    g_b1 = go_core(hopr1, [(1, 2), (2, 1)], 1)
    turn = lax.ppermute(turn, ("seq", "mp"), [(2 * a + 1, 2 * a + 0) for a in range(4)])
    hopl0, hopr0, rest0, turn = lax.optimization_barrier((hopl0, hopr0, rest0, turn))
    g_a0 = go_core(hopl0, [(0, 1), (3, 2)], 0)
    g_b0 = go_core(hopr0, [(1, 2), (2, 1)], 0)
    g_c0 = go_core(rest0, [(0, 2), (3, 1)], 0)
    own, to_a, to_c, to_b = pl.pallas_call(
        owner_kernel,
        out_shape=in_vmem(*(stack,) * 4),
        in_specs=[sm] + [vm] * 8,
        out_specs=(vm,) * 4,
        scratch_shapes=[
            *in_vmem(per_row, per_row, per_row, per_row, per_column, per_column, ((total, total), F32), wide, wide)
        ],
        compiler_params=pltpu.CompilerParams(vmem_limit_bytes=32 << 20),
        name="owner",
    )(order, *kept(turn, mine, g_c1, g_a1, g_b1, g_a0, g_b0, g_c0))
    r_a = go(to_a, [(1, 0), (2, 3)])
    r_b = go(to_b, [(1, 2), (2, 1)])
    r_c = go(to_c, [(1, 3), (2, 0)])
    return pl.pallas_call(
        unpack_kernel,
        out_shape=(jax.ShapeDtypeStruct(queries.shape, BF),) * 4,
        in_specs=[vm] * 4,
        out_specs=(anywhere,) * 4,
        scratch_shapes=[pltpu.SemaphoreType.DMA((2, 4))],
        name="unpack",
    )(*kept(own, r_a, r_c, r_b))


def solution(mesh):
    rows_columns = P(("groups", "seq"), ("head", "mp"))

    def run(span_order, queries, keys, values, grad_out):
        heads_here = queries.shape[1] // HEAD_DIM // (mesh.shape["head"] * mesh.shape["mp"])
        small = mesh.shape["seq"] == 4 and heads_here == 2
        return jax.shard_map(
            owned_per_device if small else gathered_per_device,
            mesh=mesh,
            in_specs=(P("groups"),) + (rows_columns,) * 4,
            out_specs=(rows_columns,) * 4,
            check_vma=False,
        )(span_order, queries, keys, values, grad_out)

    return run
```

```python
import functools

import jax
import jax.numpy as jnp
from jax import lax
from jax.experimental import pallas as pl
from jax.experimental.pallas import tpu as pltpu
from jax.sharding import PartitionSpec as P

HEAD_DIM = 128
SPAN = 128


def settle(values_in):
    return lax.optimization_barrier(values_in.astype(jnp.bfloat16)).astype(jnp.float32)


def masked_scores(query_block, key_block, query_pos, key_positions, factor):
    raw = (
        jnp.einsum("qhd,khd->hqk", query_block, key_block, preferred_element_type=jnp.float32)
        * factor
    )
    return jnp.where(key_positions[None, None, :] <= query_pos[None, :, None], raw, -jnp.inf)


def split_blocks(arrays, block_rows):
    count_blocks = arrays[0].shape[0] // block_rows
    stacked = tuple(
        (member.reshape((count_blocks, block_rows) + member.shape[1:]) for member in arrays)
    )
    starts = jnp.arange(count_blocks, dtype=jnp.int32) * block_rows
    return (stacked, starts)


def gathered_per_device(span_order, queries, keys, values, grad_out):
    q_rows, k_rows, v_rows, g_rows = (queries, keys, values, grad_out)
    my_rows = q_rows.shape[0]
    heads_here = q_rows.shape[1] // HEAD_DIM
    factor = HEAD_DIM ** (-0.5)
    total_rows = span_order.shape[0] * SPAN
    offsets = jnp.arange(total_rows, dtype=jnp.int32)
    all_pos = jnp.repeat(span_order, SPAN, total_repeat_length=total_rows) * SPAN + offsets % SPAN
    my_start = lax.axis_index("seq") * my_rows
    my_pos = lax.dynamic_slice_in_dim(all_pos, my_start, my_rows)
    my_q = q_rows.reshape(my_rows, heads_here, HEAD_DIM)
    my_k = k_rows.reshape(my_rows, heads_here, HEAD_DIM)
    my_v = v_rows.reshape(my_rows, heads_here, HEAD_DIM)
    my_g = g_rows.reshape(my_rows, heads_here, HEAD_DIM)

    def key_block_rows():
        return 512

    start_state = (
        jnp.full((heads_here, my_rows), -jnp.inf, jnp.float32),
        jnp.zeros((heads_here, my_rows), jnp.float32),
        jnp.zeros((heads_here, my_rows, HEAD_DIM), jnp.float32),
    )
    carry = start_state
    block_rows = key_block_rows()
    stacked, starts = split_blocks(
        (
            lax.all_gather(k_rows, "seq", axis=0, tiled=True),
            lax.all_gather(v_rows, "seq", axis=0, tiled=True),
        ),
        block_rows,
    )

    def forward_one_block(state, item):
        key_block, value_block, block_start = item
        key3 = key_block.reshape(block_rows, heads_here, HEAD_DIM)
        value3 = value_block.reshape(block_rows, heads_here, HEAD_DIM)
        positions = lax.dynamic_slice_in_dim(all_pos, block_start, block_rows)
        row_max, weight_sum, accum = state
        scores = masked_scores(my_q, key3, my_pos, positions, factor)
        new_max = jnp.maximum(row_max, jnp.max(scores, axis=2))
        safe_max = jnp.where(jnp.isfinite(new_max), new_max, 0.0)
        weights = jnp.exp(scores - safe_max[:, :, None])
        shrink = jnp.exp(row_max - safe_max)
        weight_sum = weight_sum * shrink + jnp.sum(weights, axis=2)
        accum = accum * shrink[:, :, None] + jnp.einsum(
            "hqk,khd->hqd", weights, value3.astype(jnp.float32)
        )
        return ((new_max, weight_sum, accum), None)

    carry, unused = lax.scan(forward_one_block, carry, stacked + (starts,))
    row_max, weight_sum, accum = carry
    lse_rows = (row_max + jnp.log(weight_sum)).T
    attended3 = jnp.transpose(accum / weight_sum[:, :, None], (1, 0, 2)).astype(jnp.bfloat16)
    delta_rows = jnp.sum(my_g.astype(jnp.float32) * attended3.astype(jnp.float32), axis=2)
    lse_all, delta_all = (
        lax.all_gather(lse_rows, "seq", axis=0, tiled=True),
        lax.all_gather(delta_rows, "seq", axis=0, tiled=True),
    )

    def pair_terms(
        q_block, g_block, lse_block, delta_block, q_pos, key_block, value_block, key_positions
    ):
        scores = masked_scores(q_block, key_block, q_pos, key_positions, factor)
        probs = jnp.exp(scores - lse_block.T[:, :, None])
        dprobs = jnp.einsum(
            "qhd,khd->hqk", g_block, value_block, preferred_element_type=jnp.float32
        )
        dscores = (probs * (dprobs - delta_block.T[:, :, None])).astype(jnp.bfloat16)
        return (probs.astype(jnp.bfloat16), dscores)

    def query_part(acc_q, key3, value3, positions):
        unused, dscores = pair_terms(
            my_q, my_g, lse_rows, delta_rows, my_pos, key3, value3, positions
        )
        return acc_q + jnp.einsum("hqk,khd->hqd", dscores, key3, preferred_element_type=jnp.float32)

    def key_part(acc_kv, q3, g3, block_start):
        positions = lax.dynamic_slice_in_dim(all_pos, block_start, my_rows)
        lse_block = lax.dynamic_slice_in_dim(lse_all, block_start, my_rows, 0)
        delta_block = lax.dynamic_slice_in_dim(delta_all, block_start, my_rows, 0)
        grad_k, grad_v = acc_kv
        probs_half, dscores = pair_terms(
            q3, g3, lse_block, delta_block, positions, my_k, my_v, my_pos
        )
        grad_k = grad_k + settle(
            jnp.einsum("hqk,qhd->khd", dscores, q3, preferred_element_type=jnp.float32) * factor
        )
        grad_v = grad_v + settle(
            jnp.einsum("hqk,qhd->khd", probs_half, g3, preferred_element_type=jnp.float32)
        )
        return (grad_k, grad_v)

    zeros_q = jnp.zeros((heads_here, my_rows, HEAD_DIM), jnp.float32)
    zeros_k = jnp.zeros((my_rows, heads_here, HEAD_DIM), jnp.float32)
    carry = zeros_q
    query_block_rows = key_block_rows()
    stacked, starts = split_blocks(
        (
            lax.all_gather(k_rows, "seq", axis=0, tiled=True),
            lax.all_gather(v_rows, "seq", axis=0, tiled=True),
        ),
        query_block_rows,
    )

    def query_one_block(state, item):
        key_block, value_block, block_start = item
        positions = lax.dynamic_slice_in_dim(all_pos, block_start, query_block_rows)
        key3 = key_block.reshape(query_block_rows, heads_here, HEAD_DIM)
        value3 = value_block.reshape(query_block_rows, heads_here, HEAD_DIM)
        return (query_part(state, key3, value3, positions), None)

    carry, unused = lax.scan(query_one_block, carry, stacked + (starts,))
    grad_q_acc = carry
    carry = (zeros_k, zeros_k)
    stacked, starts = split_blocks(
        (
            lax.all_gather(q_rows, "seq", axis=0, tiled=True),
            lax.all_gather(g_rows, "seq", axis=0, tiled=True),
        ),
        my_rows,
    )

    def key_one_block(state, item):
        query_block, cotangent_block, block_start = item
        q3 = query_block.reshape(my_rows, heads_here, HEAD_DIM)
        g3 = cotangent_block.reshape(my_rows, heads_here, HEAD_DIM)
        return (key_part(state, q3, g3, block_start), None)

    carry, unused = lax.scan(key_one_block, carry, stacked + (starts,))
    grad_k_acc, grad_v_acc = carry
    attended_rows = attended3.reshape(my_rows, heads_here * HEAD_DIM)
    grad_q_rows = (
        (jnp.transpose(grad_q_acc, (1, 0, 2)) * factor)
        .astype(jnp.bfloat16)
        .reshape(my_rows, heads_here * HEAD_DIM)
    )
    grad_k_rows = grad_k_acc.astype(jnp.bfloat16).reshape(my_rows, heads_here * HEAD_DIM)
    grad_v_rows = grad_v_acc.astype(jnp.bfloat16).reshape(my_rows, heads_here * HEAD_DIM)
    return (attended_rows, grad_q_rows, grad_k_rows, grad_v_rows)


F32 = jnp.float32
BF = jnp.bfloat16
NN = (((1,), (0,)), ((), ()))
NT = (((1,), (1,)), ((), ()))
LOG2E = 1.4426950408889634
FACTOR = HEAD_DIM**-0.5
BLOCK = 512
HALF = 256


def dot(a, b, dims):
    return lax.dot_general(a, b, dims, preferred_element_type=F32)


def place_here():
    me = lax.axis_index("seq")
    side = lax.div(me, 2)
    owner = (me == 1) | (me == 2)
    return me, side, owner


def columns(half):
    return pl.ds(pl.multiple_of(half * HEAD_DIM, HEAD_DIM), HEAD_DIM)


def run_copies(copies):
    for one in copies:
        one.start()
    for one in copies:
        one.wait()


def owner_kernel(order_ref, turn, own, s_c1, s_a1, s_b1, s_a0, s_b0, s_c0, o_own, o_a, o_c, o_b, q, k, v, g, kt, vt, s, dk, dv):
    me, side, held = place_here()
    rows = own.shape[0] // 4
    total = 4 * rows
    per = rows // SPAN
    near_at, far_at = 3 * side, 3 - 3 * side
    slots_out = ((me, o_own), (near_at, o_a), (far_at, o_c), (3 - me, o_b))

    @pl.when(held)
    def _():
        places = lambda slots: [
            (ref, e, pl.ds(pl.multiple_of(order_ref[at * per + e] * SPAN, SPAN), SPAN))
            for at, ref in slots
            for e in range(per)
        ]
        part = lambda n, e: slice(n * rows + e * SPAN, n * rows + (e + 1) * SPAN)
        def collect(slots):
            for src, e, where in places(slots):
                for n, to in enumerate((q, k, v, g)):
                    to[where, :] = src[part(n, e), :]

        for core, arrived in enumerate((
            ((me, own), (far_at, s_c0), (near_at, s_a0), (3 - me, s_b0)),
            ((me, own), (far_at, s_c1), (near_at, s_a1), (3 - me, s_b1)),
        )):
            pl.when(lax.axis_index("mp") == core)(functools.partial(collect, arrived))
        key_at = lax.broadcasted_iota(jnp.int32, (HALF, HALF), 0)
        query_at = lax.broadcasted_iota(jnp.int32, (HALF, HALF), 1)
        seen = key_at <= query_at
        tail = lambda whole, part: jnp.concatenate([whole[:, :HALF], part(whole[:, HALF:])], axis=1)
        stages = []
        for i in range(total // BLOCK):
            lo = slice(i * BLOCK, i * BLOCK + HALF)
            hi = slice(i * BLOCK + HALF, (i + 1) * BLOCK)
            ri = slice(i * BLOCK, (i + 1) * BLOCK)
            olds = [slice(j * BLOCK, (j + 1) * BLOCK) for j in range(i)] + [lo]
            kt[:, ri] = k[ri, :].T
            vt[:, ri] = v[ri, :].T
            qb = q[ri, :]
            qh = q[hi, :]
            top = None
            for rj in olds:
                sj = dot(k[rj, :], qb, NT) * (FACTOR * LOG2E)
                if rj is lo:
                    sj = jnp.concatenate([jnp.where(seen, sj[:, :HALF], -1e30), sj[:, HALF:]], axis=1)
                s[rj, ri] = sj
                tj = jnp.max(sj, axis=0, keepdims=True)
                top = tj if top is None else jnp.maximum(top, tj)
            sh = jnp.where(seen, dot(k[hi, :], qh, NT) * (FACTOR * LOG2E), -1e30)
            s[hi, hi] = sh
            top = tail(top, lambda x: jnp.maximum(x, jnp.max(sh, axis=0, keepdims=True)))
            stages.append((lo, hi, ri, olds, qb, qh, top))
        later = []
        for lo, hi, ri, olds, qb, qh, top in stages:
            weight, acc = None, None
            for rj in olds:
                pj = jnp.exp2(s[rj, ri] - top)
                s[rj, ri] = pj
                lj = jnp.sum(pj, axis=0, keepdims=True)
                oj = dot(vt[:, rj], pj.astype(BF), NN)
                weight = lj if weight is None else weight + lj
                acc = oj if acc is None else acc + oj
            ph = jnp.exp2(s[hi, hi] - top[:, HALF:])
            s[hi, hi] = ph
            weight = tail(weight, lambda x: x + jnp.sum(ph, axis=0, keepdims=True))
            acc = tail(acc, lambda x: x + dot(vt[:, hi], ph.astype(BF), NN))
            inverse = 1.0 / weight
            ob = (acc * inverse).astype(BF)
            gt = g[ri, :].T.astype(F32) * inverse
            gb = gt.astype(BF)
            delta = jnp.sum(gt * ob.astype(F32), axis=0, keepdims=True)
            acc = None
            for rj in olds:
                dp = dot(v[rj, :], gb, NN)
                pj = s[rj, ri]
                ds = (pj * (dp - delta)).astype(BF)
                vj = dot(pj.astype(BF), gb, NT)
                kj = dot(ds, qb, NN)
                if rj is lo:
                    dv[rj, :] = vj
                    dk[rj, :] = kj
                else:
                    dv[rj, :] += vj
                    dk[rj, :] += kj
                qj = dot(kt[:, rj], ds, NN)
                acc = qj if acc is None else acc + qj
            dp = dot(v[hi, :], gb[:, HALF:], NN)
            ph = s[hi, hi]
            ds = (ph * (dp - delta[:, HALF:])).astype(BF)
            dv[hi, :] = dot(ph.astype(BF), gb[:, HALF:], NT)
            dk[hi, :] = dot(ds, qh, NN)
            acc = tail(acc, lambda x: x + dot(kt[:, hi], ds, NN))
            q[ri, :] = (acc * FACTOR).astype(BF).T
            g[ri, :] = ob.T
        for dst, e, where in places(slots_out):
            dst[part(0, e), :] = g[where, :]
            dst[part(1, e), :] = q[where, :]
            dst[part(2, e), :] = (dk[where, :] * FACTOR).astype(BF)
            dst[part(3, e), :] = dv[where, :].astype(BF)


def pack_kernel(order, q, k, v, g, rest1, outer1, cross1, outer0, cross0, rest0, mine, turn, order_out, sem, order_sem):
    sh = q.shape[0]
    _, side, owner = place_here()
    turn[...] = jnp.zeros_like(turn)
    for core, outer, cross, rest in ((0, outer0, cross0, rest0), (1, outer1, cross1, rest1)):
        for held, halves in ((True, ((cross, 1 - side), (mine, side))), (False, ((rest, 1 - side), (outer, side)))):
            @pl.when((lax.axis_index("mp") == core) & (owner == held))
            def _():
                run_copies([
                    pltpu.make_async_copy(src.at[:, columns(half)], dst.at[n * sh:(n + 1) * sh, :], sem.at[m, n])
                    for m, (dst, half) in enumerate(halves)
                    for n, src in enumerate((q, k, v, g))
                ] + [pltpu.make_async_copy(order, order_out, order_sem)])


def unpack_kernel(own, r_a, r_c, r_b, *refs):
    outs, sem = refs[:4], refs[4]
    sh = outs[0].shape[0]
    me, side, _ = place_here()
    for at, near, far in ((0, r_a, r_c), (1, own, r_b), (2, own, r_b), (3, r_a, r_c)):
        @pl.when(me == at)
        def _():
            run_copies([
                pltpu.make_async_copy(src.at[n * sh:(n + 1) * sh, :], dst.at[:, columns(half)], sem.at[m, n])
                for m, (src, half) in enumerate(((far, 1 - side), (near, side)))
                for n, dst in enumerate(outs)
            ])


def in_vmem(*shapes):
    return tuple(pltpu.VMEM(shape, dtype) for shape, dtype in shapes)


def kept(*arrays):
    return tuple(pltpu.with_memory_space_constraint(x, pltpu.VMEM) for x in arrays)


def owned_per_device(span_order, queries, keys, values, grad_out):
    rows = queries.shape[0]
    total = 4 * rows
    anywhere = pl.BlockSpec(memory_space=pl.ANY)
    vm = pl.BlockSpec(memory_space=pltpu.VMEM)
    sm = pl.BlockSpec(memory_space=pltpu.SMEM)
    stack = ((4 * rows, HEAD_DIM), BF)
    per_row = ((total, HEAD_DIM), BF)
    per_column = ((HEAD_DIM, total), BF)
    wide = ((total, HEAD_DIM), F32)
    rest1, outer1, cross1, outer0, cross0, rest0, mine, turn, order = pl.pallas_call(
        pack_kernel,
        out_shape=in_vmem(*(stack,) * 7, ((16, HEAD_DIM), BF)) + (pltpu.SMEM(span_order.shape, span_order.dtype),),
        in_specs=[anywhere] * 5,
        out_specs=(vm,) * 8 + (sm,),
        scratch_shapes=[pltpu.SemaphoreType.DMA((2, 4)), pltpu.SemaphoreType.DMA],
        name="pack",
    )(span_order, queries, keys, values, grad_out)
    go = lambda x, pairs: lax.ppermute(x, "seq", pairs)

    def go_core(x, pairs, core):
        return lax.ppermute(x, ("seq", "mp"), [(2 * a + core, 2 * b + core) for a, b in pairs])

    g_c1 = go_core(rest1, [(0, 2), (3, 1)], 1)
    g_a1 = go_core(outer1, [(0, 1), (3, 2)], 1)
    g_b1 = go_core(cross1, [(1, 2), (2, 1)], 1)
    turn = lax.ppermute(turn, ("seq", "mp"), [(2 * a + 1, 2 * a + 0) for a in range(4)])
    outer0, cross0, rest0, turn = lax.optimization_barrier((outer0, cross0, rest0, turn))
    g_a0 = go_core(outer0, [(0, 1), (3, 2)], 0)
    g_b0 = go_core(cross0, [(1, 2), (2, 1)], 0)
    g_c0 = go_core(rest0, [(0, 2), (3, 1)], 0)
    own, to_a, to_c, to_b = pl.pallas_call(
        owner_kernel,
        out_shape=in_vmem(*(stack,) * 4),
        in_specs=[sm] + [vm] * 8,
        out_specs=(vm,) * 4,
        scratch_shapes=[
            *in_vmem(per_row, per_row, per_row, per_row, per_column, per_column, ((total, total), F32), wide, wide)
        ],
        compiler_params=pltpu.CompilerParams(vmem_limit_bytes=32 << 20),
        name="owner",
    )(order, *kept(turn, mine, g_c1, g_a1, g_b1, g_a0, g_b0, g_c0))
    r_a = go(to_a, [(1, 0), (2, 3)])
    r_b = go(to_b, [(1, 2), (2, 1)])
    r_c = go(to_c, [(1, 3), (2, 0)])
    return pl.pallas_call(
        unpack_kernel,
        out_shape=(jax.ShapeDtypeStruct(queries.shape, BF),) * 4,
        in_specs=[vm] * 4,
        out_specs=(anywhere,) * 4,
        scratch_shapes=[pltpu.SemaphoreType.DMA((2, 4))],
        name="unpack",
    )(*kept(own, r_a, r_c, r_b))


def solution(mesh):
    rows_columns = P(("groups", "seq"), ("head", "mp"))

    def run(span_order, queries, keys, values, grad_out):
        heads_here = queries.shape[1] // HEAD_DIM // (mesh.shape["head"] * mesh.shape["mp"])
        small = mesh.shape["seq"] == 4 and heads_here == 2
        return jax.shard_map(
            owned_per_device if small else gathered_per_device,
            mesh=mesh,
            in_specs=(P("groups"),) + (rows_columns,) * 4,
            out_specs=(rows_columns,) * 4,
            check_vma=False,
        )(span_order, queries, keys, values, grad_out)

    return run
```

```python
import functools

import jax
import jax.numpy as jnp
from jax import lax
from jax.experimental import pallas as pl
from jax.experimental.pallas import tpu as pltpu
from jax.sharding import PartitionSpec as P

HEAD_DIM = 128
SPAN = 128


def settle(values_in):
    return lax.optimization_barrier(values_in.astype(jnp.bfloat16)).astype(jnp.float32)


def masked_scores(query_block, key_block, query_pos, key_positions, factor):
    raw = (
        jnp.einsum("qhd,khd->hqk", query_block, key_block, preferred_element_type=jnp.float32)
        * factor
    )
    return jnp.where(key_positions[None, None, :] <= query_pos[None, :, None], raw, -jnp.inf)


def split_blocks(arrays, block_rows):
    count_blocks = arrays[0].shape[0] // block_rows
    stacked = tuple(
        (member.reshape((count_blocks, block_rows) + member.shape[1:]) for member in arrays)
    )
    starts = jnp.arange(count_blocks, dtype=jnp.int32) * block_rows
    return (stacked, starts)


def gathered_per_device(span_order, queries, keys, values, grad_out):
    q_rows, k_rows, v_rows, g_rows = (queries, keys, values, grad_out)
    my_rows = q_rows.shape[0]
    heads_here = q_rows.shape[1] // HEAD_DIM
    factor = HEAD_DIM ** (-0.5)
    total_rows = span_order.shape[0] * SPAN
    offsets = jnp.arange(total_rows, dtype=jnp.int32)
    all_pos = jnp.repeat(span_order, SPAN, total_repeat_length=total_rows) * SPAN + offsets % SPAN
    my_start = lax.axis_index("seq") * my_rows
    my_pos = lax.dynamic_slice_in_dim(all_pos, my_start, my_rows)
    my_q = q_rows.reshape(my_rows, heads_here, HEAD_DIM)
    my_k = k_rows.reshape(my_rows, heads_here, HEAD_DIM)
    my_v = v_rows.reshape(my_rows, heads_here, HEAD_DIM)
    my_g = g_rows.reshape(my_rows, heads_here, HEAD_DIM)

    def key_block_rows():
        return 512

    start_state = (
        jnp.full((heads_here, my_rows), -jnp.inf, jnp.float32),
        jnp.zeros((heads_here, my_rows), jnp.float32),
        jnp.zeros((heads_here, my_rows, HEAD_DIM), jnp.float32),
    )
    carry = start_state
    block_rows = key_block_rows()
    stacked, starts = split_blocks(
        (
            lax.all_gather(k_rows, "seq", axis=0, tiled=True),
            lax.all_gather(v_rows, "seq", axis=0, tiled=True),
        ),
        block_rows,
    )

    def forward_one_block(state, item):
        key_block, value_block, block_start = item
        key3 = key_block.reshape(block_rows, heads_here, HEAD_DIM)
        value3 = value_block.reshape(block_rows, heads_here, HEAD_DIM)
        positions = lax.dynamic_slice_in_dim(all_pos, block_start, block_rows)
        row_max, weight_sum, accum = state
        scores = masked_scores(my_q, key3, my_pos, positions, factor)
        new_max = jnp.maximum(row_max, jnp.max(scores, axis=2))
        safe_max = jnp.where(jnp.isfinite(new_max), new_max, 0.0)
        weights = jnp.exp(scores - safe_max[:, :, None])
        shrink = jnp.exp(row_max - safe_max)
        weight_sum = weight_sum * shrink + jnp.sum(weights, axis=2)
        accum = accum * shrink[:, :, None] + jnp.einsum(
            "hqk,khd->hqd", weights, value3.astype(jnp.float32)
        )
        return ((new_max, weight_sum, accum), None)

    carry, unused = lax.scan(forward_one_block, carry, stacked + (starts,))
    row_max, weight_sum, accum = carry
    lse_rows = (row_max + jnp.log(weight_sum)).T
    attended3 = jnp.transpose(accum / weight_sum[:, :, None], (1, 0, 2)).astype(jnp.bfloat16)
    delta_rows = jnp.sum(my_g.astype(jnp.float32) * attended3.astype(jnp.float32), axis=2)
    lse_all, delta_all = (
        lax.all_gather(lse_rows, "seq", axis=0, tiled=True),
        lax.all_gather(delta_rows, "seq", axis=0, tiled=True),
    )

    def pair_terms(
        q_block, g_block, lse_block, delta_block, q_pos, key_block, value_block, key_positions
    ):
        scores = masked_scores(q_block, key_block, q_pos, key_positions, factor)
        probs = jnp.exp(scores - lse_block.T[:, :, None])
        dprobs = jnp.einsum(
            "qhd,khd->hqk", g_block, value_block, preferred_element_type=jnp.float32
        )
        dscores = (probs * (dprobs - delta_block.T[:, :, None])).astype(jnp.bfloat16)
        return (probs.astype(jnp.bfloat16), dscores)

    def query_part(acc_q, key3, value3, positions):
        unused, dscores = pair_terms(
            my_q, my_g, lse_rows, delta_rows, my_pos, key3, value3, positions
        )
        return acc_q + jnp.einsum("hqk,khd->hqd", dscores, key3, preferred_element_type=jnp.float32)

    def key_part(acc_kv, q3, g3, block_start):
        positions = lax.dynamic_slice_in_dim(all_pos, block_start, my_rows)
        lse_block = lax.dynamic_slice_in_dim(lse_all, block_start, my_rows, 0)
        delta_block = lax.dynamic_slice_in_dim(delta_all, block_start, my_rows, 0)
        grad_k, grad_v = acc_kv
        probs_half, dscores = pair_terms(
            q3, g3, lse_block, delta_block, positions, my_k, my_v, my_pos
        )
        grad_k = grad_k + settle(
            jnp.einsum("hqk,qhd->khd", dscores, q3, preferred_element_type=jnp.float32) * factor
        )
        grad_v = grad_v + settle(
            jnp.einsum("hqk,qhd->khd", probs_half, g3, preferred_element_type=jnp.float32)
        )
        return (grad_k, grad_v)

    zeros_q = jnp.zeros((heads_here, my_rows, HEAD_DIM), jnp.float32)
    zeros_k = jnp.zeros((my_rows, heads_here, HEAD_DIM), jnp.float32)
    carry = zeros_q
    query_block_rows = key_block_rows()
    stacked, starts = split_blocks(
        (
            lax.all_gather(k_rows, "seq", axis=0, tiled=True),
            lax.all_gather(v_rows, "seq", axis=0, tiled=True),
        ),
        query_block_rows,
    )

    def query_one_block(state, item):
        key_block, value_block, block_start = item
        positions = lax.dynamic_slice_in_dim(all_pos, block_start, query_block_rows)
        key3 = key_block.reshape(query_block_rows, heads_here, HEAD_DIM)
        value3 = value_block.reshape(query_block_rows, heads_here, HEAD_DIM)
        return (query_part(state, key3, value3, positions), None)

    carry, unused = lax.scan(query_one_block, carry, stacked + (starts,))
    grad_q_acc = carry
    carry = (zeros_k, zeros_k)
    stacked, starts = split_blocks(
        (
            lax.all_gather(q_rows, "seq", axis=0, tiled=True),
            lax.all_gather(g_rows, "seq", axis=0, tiled=True),
        ),
        my_rows,
    )

    def key_one_block(state, item):
        query_block, cotangent_block, block_start = item
        q3 = query_block.reshape(my_rows, heads_here, HEAD_DIM)
        g3 = cotangent_block.reshape(my_rows, heads_here, HEAD_DIM)
        return (key_part(state, q3, g3, block_start), None)

    carry, unused = lax.scan(key_one_block, carry, stacked + (starts,))
    grad_k_acc, grad_v_acc = carry
    attended_rows = attended3.reshape(my_rows, heads_here * HEAD_DIM)
    grad_q_rows = (
        (jnp.transpose(grad_q_acc, (1, 0, 2)) * factor)
        .astype(jnp.bfloat16)
        .reshape(my_rows, heads_here * HEAD_DIM)
    )
    grad_k_rows = grad_k_acc.astype(jnp.bfloat16).reshape(my_rows, heads_here * HEAD_DIM)
    grad_v_rows = grad_v_acc.astype(jnp.bfloat16).reshape(my_rows, heads_here * HEAD_DIM)
    return (attended_rows, grad_q_rows, grad_k_rows, grad_v_rows)


F32 = jnp.float32
BF = jnp.bfloat16
NN = (((1,), (0,)), ((), ()))
NT = (((1,), (1,)), ((), ()))
LOG2E = 1.4426950408889634
FACTOR = HEAD_DIM**-0.5
BLOCK = 512
HALF = 256


def dot(a, b, dims):
    return lax.dot_general(a, b, dims, preferred_element_type=F32)


def place_here():
    me = lax.axis_index("seq")
    side = lax.div(me, 2)
    owner = (me == 1) | (me == 2)
    return me, side, owner


def columns(half):
    return pl.ds(pl.multiple_of(half * HEAD_DIM, HEAD_DIM), HEAD_DIM)


def run_copies(copies):
    for one in copies:
        one.start()
    for one in copies:
        one.wait()


def owner_kernel(order_ref, turn, own, s_c1, s_a1, s_b1, s_a0, s_c0, s_b0, o_own, o_a, o_c, o_b, q, k, v, g, kt, vt, s, dk, dv):
    me, side, held = place_here()
    rows = own.shape[0] // 4
    total = 4 * rows
    per = rows // SPAN
    near_at, far_at = 3 * side, 3 - 3 * side
    slots_out = ((me, o_own), (near_at, o_a), (far_at, o_c), (3 - me, o_b))

    @pl.when(held)
    def _():
        places = lambda slots: [
            (ref, e, pl.ds(pl.multiple_of(order_ref[at * per + e] * SPAN, SPAN), SPAN))
            for at, ref in slots
            for e in range(per)
        ]
        part = lambda n, e: slice(n * rows + e * SPAN, n * rows + (e + 1) * SPAN)
        def collect(slots):
            for src, e, where in places(slots):
                for n, to in enumerate((q, k, v, g)):
                    to[where, :] = src[part(n, e), :]

        for core, arrived in enumerate((
            ((me, own), (far_at, s_c0), (near_at, s_a0), (3 - me, s_b0)),
            ((me, own), (far_at, s_c1), (near_at, s_a1), (3 - me, s_b1)),
        )):
            pl.when(lax.axis_index("mp") == core)(functools.partial(collect, arrived))
        key_at = lax.broadcasted_iota(jnp.int32, (HALF, HALF), 0)
        query_at = lax.broadcasted_iota(jnp.int32, (HALF, HALF), 1)
        seen = key_at <= query_at
        tail = lambda whole, part: jnp.concatenate([whole[:, :HALF], part(whole[:, HALF:])], axis=1)
        stages = []
        for i in range(total // BLOCK):
            lo = slice(i * BLOCK, i * BLOCK + HALF)
            hi = slice(i * BLOCK + HALF, (i + 1) * BLOCK)
            ri = slice(i * BLOCK, (i + 1) * BLOCK)
            olds = [slice(j * BLOCK, (j + 1) * BLOCK) for j in range(i)] + [lo]
            kt[:, ri] = k[ri, :].T
            vt[:, ri] = v[ri, :].T
            qb = q[ri, :]
            qh = q[hi, :]
            top = None
            for rj in olds:
                sj = dot(k[rj, :], qb, NT) * (FACTOR * LOG2E)
                if rj is lo:
                    sj = jnp.concatenate([jnp.where(seen, sj[:, :HALF], -1e30), sj[:, HALF:]], axis=1)
                s[rj, ri] = sj
                tj = jnp.max(sj, axis=0, keepdims=True)
                top = tj if top is None else jnp.maximum(top, tj)
            sh = jnp.where(seen, dot(k[hi, :], qh, NT) * (FACTOR * LOG2E), -1e30)
            s[hi, hi] = sh
            top = tail(top, lambda x: jnp.maximum(x, jnp.max(sh, axis=0, keepdims=True)))
            stages.append((lo, hi, ri, olds, qb, qh, top))
        later = []
        for lo, hi, ri, olds, qb, qh, top in stages:
            weight, acc = None, None
            for rj in olds:
                pj = jnp.exp2(s[rj, ri] - top)
                s[rj, ri] = pj
                lj = jnp.sum(pj, axis=0, keepdims=True)
                oj = dot(vt[:, rj], pj.astype(BF), NN)
                weight = lj if weight is None else weight + lj
                acc = oj if acc is None else acc + oj
            ph = jnp.exp2(s[hi, hi] - top[:, HALF:])
            s[hi, hi] = ph
            weight = tail(weight, lambda x: x + jnp.sum(ph, axis=0, keepdims=True))
            acc = tail(acc, lambda x: x + dot(vt[:, hi], ph.astype(BF), NN))
            inverse = 1.0 / weight
            ob = (acc * inverse).astype(BF)
            gt = g[ri, :].T.astype(F32) * inverse
            gb = gt.astype(BF)
            delta = jnp.sum(gt * ob.astype(F32), axis=0, keepdims=True)
            acc = None
            for rj in olds:
                dp = dot(v[rj, :], gb, NN)
                pj = s[rj, ri]
                ds = (pj * (dp - delta)).astype(BF)
                vj = dot(pj.astype(BF), gb, NT)
                kj = dot(ds, qb, NN)
                if rj is lo:
                    dv[rj, :] = vj
                    dk[rj, :] = kj
                else:
                    dv[rj, :] += vj
                    dk[rj, :] += kj
                qj = dot(kt[:, rj], ds, NN)
                acc = qj if acc is None else acc + qj
            dp = dot(v[hi, :], gb[:, HALF:], NN)
            ph = s[hi, hi]
            ds = (ph * (dp - delta[:, HALF:])).astype(BF)
            dv[hi, :] = dot(ph.astype(BF), gb[:, HALF:], NT)
            dk[hi, :] = dot(ds, qh, NN)
            acc = tail(acc, lambda x: x + dot(kt[:, hi], ds, NN))
            q[ri, :] = (acc * FACTOR).astype(BF).T
            g[ri, :] = ob.T
        for dst, e, where in places(slots_out):
            dst[part(0, e), :] = g[where, :]
            dst[part(1, e), :] = q[where, :]
            dst[part(2, e), :] = (dk[where, :] * FACTOR).astype(BF)
            dst[part(3, e), :] = dv[where, :].astype(BF)


def pack_kernel(order, q, k, v, g, rest1, outer1, cross1, outer0, cross0, rest0, mine, turn, order_out, sem, order_sem):
    sh = q.shape[0]
    _, side, owner = place_here()
    turn[...] = jnp.zeros_like(turn)
    for core, outer, cross, rest in ((0, outer0, cross0, rest0), (1, outer1, cross1, rest1)):
        for held, halves in ((True, ((cross, 1 - side), (mine, side))), (False, ((rest, 1 - side), (outer, side)))):
            @pl.when((lax.axis_index("mp") == core) & (owner == held))
            def _():
                run_copies([
                    pltpu.make_async_copy(src.at[:, columns(half)], dst.at[n * sh:(n + 1) * sh, :], sem.at[m, n])
                    for m, (dst, half) in enumerate(halves)
                    for n, src in enumerate((q, k, v, g))
                ] + [pltpu.make_async_copy(order, order_out, order_sem)])


def unpack_kernel(own, r_a, r_c, r_b, *refs):
    outs, sem = refs[:4], refs[4]
    sh = outs[0].shape[0]
    me, side, _ = place_here()
    for at, near, far in ((0, r_a, r_c), (1, own, r_b), (2, own, r_b), (3, r_a, r_c)):
        @pl.when(me == at)
        def _():
            run_copies([
                pltpu.make_async_copy(src.at[n * sh:(n + 1) * sh, :], dst.at[:, columns(half)], sem.at[m, n])
                for m, (src, half) in enumerate(((far, 1 - side), (near, side)))
                for n, dst in enumerate(outs)
            ])


def in_vmem(*shapes):
    return tuple(pltpu.VMEM(shape, dtype) for shape, dtype in shapes)


def kept(*arrays):
    return tuple(pltpu.with_memory_space_constraint(x, pltpu.VMEM) for x in arrays)


def owned_per_device(span_order, queries, keys, values, grad_out):
    rows = queries.shape[0]
    total = 4 * rows
    anywhere = pl.BlockSpec(memory_space=pl.ANY)
    vm = pl.BlockSpec(memory_space=pltpu.VMEM)
    sm = pl.BlockSpec(memory_space=pltpu.SMEM)
    stack = ((4 * rows, HEAD_DIM), BF)
    per_row = ((total, HEAD_DIM), BF)
    per_column = ((HEAD_DIM, total), BF)
    wide = ((total, HEAD_DIM), F32)
    rest1, outer1, cross1, outer0, cross0, rest0, mine, turn, order = pl.pallas_call(
        pack_kernel,
        out_shape=in_vmem(*(stack,) * 7, ((16, HEAD_DIM), BF)) + (pltpu.SMEM(span_order.shape, span_order.dtype),),
        in_specs=[anywhere] * 5,
        out_specs=(vm,) * 8 + (sm,),
        scratch_shapes=[pltpu.SemaphoreType.DMA((2, 4)), pltpu.SemaphoreType.DMA],
        name="pack",
    )(span_order, queries, keys, values, grad_out)
    go = lambda x, pairs: lax.ppermute(x, "seq", pairs)

    def go_core(x, pairs, core):
        return lax.ppermute(x, ("seq", "mp"), [(2 * a + core, 2 * b + core) for a, b in pairs])

    g_c1 = go_core(rest1, [(0, 2), (3, 1)], 1)
    g_a1 = go_core(outer1, [(0, 1), (3, 2)], 1)
    g_b1 = go_core(cross1, [(1, 2), (2, 1)], 1)
    turn = lax.ppermute(turn, ("seq", "mp"), [(2 * a + 1, 2 * a + 0) for a in range(4)])
    outer0, cross0, rest0, turn = lax.optimization_barrier((outer0, cross0, rest0, turn))
    g_a0 = go_core(outer0, [(0, 1), (3, 2)], 0)
    g_c0 = go_core(rest0, [(0, 2), (3, 1)], 0)
    g_b0 = go_core(cross0, [(1, 2), (2, 1)], 0)
    own, to_a, to_c, to_b = pl.pallas_call(
        owner_kernel,
        out_shape=in_vmem(*(stack,) * 4),
        in_specs=[sm] + [vm] * 8,
        out_specs=(vm,) * 4,
        scratch_shapes=[
            *in_vmem(per_row, per_row, per_row, per_row, per_column, per_column, ((total, total), F32), wide, wide)
        ],
        compiler_params=pltpu.CompilerParams(vmem_limit_bytes=32 << 20),
        name="owner",
    )(order, *kept(turn, mine, g_c1, g_a1, g_b1, g_a0, g_c0, g_b0))
    r_a = go(to_a, [(1, 0), (2, 3)])
    r_b = go(to_b, [(1, 2), (2, 1)])
    r_c = go(to_c, [(1, 3), (2, 0)])
    return pl.pallas_call(
        unpack_kernel,
        out_shape=(jax.ShapeDtypeStruct(queries.shape, BF),) * 4,
        in_specs=[vm] * 4,
        out_specs=(anywhere,) * 4,
        scratch_shapes=[pltpu.SemaphoreType.DMA((2, 4))],
        name="unpack",
    )(*kept(own, r_a, r_c, r_b))


def solution(mesh):
    rows_columns = P(("groups", "seq"), ("head", "mp"))

    def run(span_order, queries, keys, values, grad_out):
        heads_here = queries.shape[1] // HEAD_DIM // (mesh.shape["head"] * mesh.shape["mp"])
        small = mesh.shape["seq"] == 4 and heads_here == 2
        return jax.shard_map(
            owned_per_device if small else gathered_per_device,
            mesh=mesh,
            in_specs=(P("groups"),) + (rows_columns,) * 4,
            out_specs=(rows_columns,) * 4,
            check_vma=False,
        )(span_order, queries, keys, values, grad_out)

    return run
```

```python
import functools

import jax
import jax.numpy as jnp
from jax import lax
from jax.experimental import pallas as pl
from jax.experimental.pallas import tpu as pltpu
from jax.sharding import PartitionSpec as P

HEAD_DIM = 128
SPAN = 128


def settle(values_in):
    return lax.optimization_barrier(values_in.astype(jnp.bfloat16)).astype(jnp.float32)


def masked_scores(query_block, key_block, query_pos, key_positions, factor):
    raw = (
        jnp.einsum("qhd,khd->hqk", query_block, key_block, preferred_element_type=jnp.float32)
        * factor
    )
    return jnp.where(key_positions[None, None, :] <= query_pos[None, :, None], raw, -jnp.inf)


def split_blocks(arrays, block_rows):
    count_blocks = arrays[0].shape[0] // block_rows
    stacked = tuple(
        (member.reshape((count_blocks, block_rows) + member.shape[1:]) for member in arrays)
    )
    starts = jnp.arange(count_blocks, dtype=jnp.int32) * block_rows
    return (stacked, starts)


def gathered_per_device(span_order, queries, keys, values, grad_out):
    q_rows, k_rows, v_rows, g_rows = (queries, keys, values, grad_out)
    my_rows = q_rows.shape[0]
    heads_here = q_rows.shape[1] // HEAD_DIM
    factor = HEAD_DIM ** (-0.5)
    total_rows = span_order.shape[0] * SPAN
    offsets = jnp.arange(total_rows, dtype=jnp.int32)
    all_pos = jnp.repeat(span_order, SPAN, total_repeat_length=total_rows) * SPAN + offsets % SPAN
    my_start = lax.axis_index("seq") * my_rows
    my_pos = lax.dynamic_slice_in_dim(all_pos, my_start, my_rows)
    my_q = q_rows.reshape(my_rows, heads_here, HEAD_DIM)
    my_k = k_rows.reshape(my_rows, heads_here, HEAD_DIM)
    my_v = v_rows.reshape(my_rows, heads_here, HEAD_DIM)
    my_g = g_rows.reshape(my_rows, heads_here, HEAD_DIM)

    def key_block_rows():
        return 512

    start_state = (
        jnp.full((heads_here, my_rows), -jnp.inf, jnp.float32),
        jnp.zeros((heads_here, my_rows), jnp.float32),
        jnp.zeros((heads_here, my_rows, HEAD_DIM), jnp.float32),
    )
    carry = start_state
    block_rows = key_block_rows()
    stacked, starts = split_blocks(
        (
            lax.all_gather(k_rows, "seq", axis=0, tiled=True),
            lax.all_gather(v_rows, "seq", axis=0, tiled=True),
        ),
        block_rows,
    )

    def forward_one_block(state, item):
        key_block, value_block, block_start = item
        key3 = key_block.reshape(block_rows, heads_here, HEAD_DIM)
        value3 = value_block.reshape(block_rows, heads_here, HEAD_DIM)
        positions = lax.dynamic_slice_in_dim(all_pos, block_start, block_rows)
        row_max, weight_sum, accum = state
        scores = masked_scores(my_q, key3, my_pos, positions, factor)
        new_max = jnp.maximum(row_max, jnp.max(scores, axis=2))
        safe_max = jnp.where(jnp.isfinite(new_max), new_max, 0.0)
        weights = jnp.exp(scores - safe_max[:, :, None])
        shrink = jnp.exp(row_max - safe_max)
        weight_sum = weight_sum * shrink + jnp.sum(weights, axis=2)
        accum = accum * shrink[:, :, None] + jnp.einsum(
            "hqk,khd->hqd", weights, value3.astype(jnp.float32)
        )
        return ((new_max, weight_sum, accum), None)

    carry, unused = lax.scan(forward_one_block, carry, stacked + (starts,))
    row_max, weight_sum, accum = carry
    lse_rows = (row_max + jnp.log(weight_sum)).T
    attended3 = jnp.transpose(accum / weight_sum[:, :, None], (1, 0, 2)).astype(jnp.bfloat16)
    delta_rows = jnp.sum(my_g.astype(jnp.float32) * attended3.astype(jnp.float32), axis=2)
    lse_all, delta_all = (
        lax.all_gather(lse_rows, "seq", axis=0, tiled=True),
        lax.all_gather(delta_rows, "seq", axis=0, tiled=True),
    )

    def pair_terms(
        q_block, g_block, lse_block, delta_block, q_pos, key_block, value_block, key_positions
    ):
        scores = masked_scores(q_block, key_block, q_pos, key_positions, factor)
        probs = jnp.exp(scores - lse_block.T[:, :, None])
        dprobs = jnp.einsum(
            "qhd,khd->hqk", g_block, value_block, preferred_element_type=jnp.float32
        )
        dscores = (probs * (dprobs - delta_block.T[:, :, None])).astype(jnp.bfloat16)
        return (probs.astype(jnp.bfloat16), dscores)

    def query_part(acc_q, key3, value3, positions):
        unused, dscores = pair_terms(
            my_q, my_g, lse_rows, delta_rows, my_pos, key3, value3, positions
        )
        return acc_q + jnp.einsum("hqk,khd->hqd", dscores, key3, preferred_element_type=jnp.float32)

    def key_part(acc_kv, q3, g3, block_start):
        positions = lax.dynamic_slice_in_dim(all_pos, block_start, my_rows)
        lse_block = lax.dynamic_slice_in_dim(lse_all, block_start, my_rows, 0)
        delta_block = lax.dynamic_slice_in_dim(delta_all, block_start, my_rows, 0)
        grad_k, grad_v = acc_kv
        probs_half, dscores = pair_terms(
            q3, g3, lse_block, delta_block, positions, my_k, my_v, my_pos
        )
        grad_k = grad_k + settle(
            jnp.einsum("hqk,qhd->khd", dscores, q3, preferred_element_type=jnp.float32) * factor
        )
        grad_v = grad_v + settle(
            jnp.einsum("hqk,qhd->khd", probs_half, g3, preferred_element_type=jnp.float32)
        )
        return (grad_k, grad_v)

    zeros_q = jnp.zeros((heads_here, my_rows, HEAD_DIM), jnp.float32)
    zeros_k = jnp.zeros((my_rows, heads_here, HEAD_DIM), jnp.float32)
    carry = zeros_q
    query_block_rows = key_block_rows()
    stacked, starts = split_blocks(
        (
            lax.all_gather(k_rows, "seq", axis=0, tiled=True),
            lax.all_gather(v_rows, "seq", axis=0, tiled=True),
        ),
        query_block_rows,
    )

    def query_one_block(state, item):
        key_block, value_block, block_start = item
        positions = lax.dynamic_slice_in_dim(all_pos, block_start, query_block_rows)
        key3 = key_block.reshape(query_block_rows, heads_here, HEAD_DIM)
        value3 = value_block.reshape(query_block_rows, heads_here, HEAD_DIM)
        return (query_part(state, key3, value3, positions), None)

    carry, unused = lax.scan(query_one_block, carry, stacked + (starts,))
    grad_q_acc = carry
    carry = (zeros_k, zeros_k)
    stacked, starts = split_blocks(
        (
            lax.all_gather(q_rows, "seq", axis=0, tiled=True),
            lax.all_gather(g_rows, "seq", axis=0, tiled=True),
        ),
        my_rows,
    )

    def key_one_block(state, item):
        query_block, cotangent_block, block_start = item
        q3 = query_block.reshape(my_rows, heads_here, HEAD_DIM)
        g3 = cotangent_block.reshape(my_rows, heads_here, HEAD_DIM)
        return (key_part(state, q3, g3, block_start), None)

    carry, unused = lax.scan(key_one_block, carry, stacked + (starts,))
    grad_k_acc, grad_v_acc = carry
    attended_rows = attended3.reshape(my_rows, heads_here * HEAD_DIM)
    grad_q_rows = (
        (jnp.transpose(grad_q_acc, (1, 0, 2)) * factor)
        .astype(jnp.bfloat16)
        .reshape(my_rows, heads_here * HEAD_DIM)
    )
    grad_k_rows = grad_k_acc.astype(jnp.bfloat16).reshape(my_rows, heads_here * HEAD_DIM)
    grad_v_rows = grad_v_acc.astype(jnp.bfloat16).reshape(my_rows, heads_here * HEAD_DIM)
    return (attended_rows, grad_q_rows, grad_k_rows, grad_v_rows)


F32 = jnp.float32
BF = jnp.bfloat16
NN = (((1,), (0,)), ((), ()))
NT = (((1,), (1,)), ((), ()))
LOG2E = 1.4426950408889634
FACTOR = HEAD_DIM**-0.5
BLOCK = 512
HALF = 256


def dot(a, b, dims):
    return lax.dot_general(a, b, dims, preferred_element_type=F32)


def place_here():
    me = lax.axis_index("seq")
    side = lax.div(me, 2)
    owner = (me == 1) | (me == 2)
    return me, side, owner


def columns(half):
    return pl.ds(pl.multiple_of(half * HEAD_DIM, HEAD_DIM), HEAD_DIM)


def run_copies(copies):
    for one in copies:
        one.start()
    for one in copies:
        one.wait()


def owner_kernel(order_ref, turn, own, s_c1, s_a1, s_b1, s_a0, s_c0, s_b0, o_own, o_a, o_c, o_b, q, k, v, g, kt, vt, s, dk, dv):
    me, side, held = place_here()
    rows = own.shape[0] // 4
    total = 4 * rows
    per = rows // SPAN
    near_at, far_at = 3 * side, 3 - 3 * side
    slots_out = ((me, o_own), (near_at, o_a), (far_at, o_c), (3 - me, o_b))

    @pl.when(held)
    def _():
        places = lambda slots: [
            (ref, e, pl.ds(pl.multiple_of(order_ref[at * per + e] * SPAN, SPAN), SPAN))
            for at, ref in slots
            for e in range(per)
        ]
        part = lambda n, e: slice(n * rows + e * SPAN, n * rows + (e + 1) * SPAN)
        def collect(slots):
            for src, e, where in places(slots):
                for n, to in enumerate((q, k, v, g)):
                    to[where, :] = src[part(n, e), :]

        for core, arrived in enumerate((
            ((me, own), (far_at, s_c0), (near_at, s_a0), (3 - me, s_b0)),
            ((me, own), (far_at, s_c1), (near_at, s_a1), (3 - me, s_b1)),
        )):
            pl.when(lax.axis_index("mp") == core)(functools.partial(collect, arrived))
        key_at = lax.broadcasted_iota(jnp.int32, (HALF, HALF), 0)
        query_at = lax.broadcasted_iota(jnp.int32, (HALF, HALF), 1)
        seen = key_at <= query_at
        tail = lambda whole, part: jnp.concatenate([whole[:, :HALF], part(whole[:, HALF:])], axis=1)
        stages = []
        for i in range(total // BLOCK):
            lo = slice(i * BLOCK, i * BLOCK + HALF)
            hi = slice(i * BLOCK + HALF, (i + 1) * BLOCK)
            ri = slice(i * BLOCK, (i + 1) * BLOCK)
            olds = [slice(j * BLOCK, (j + 1) * BLOCK) for j in range(i)] + [lo]
            kt[:, ri] = k[ri, :].T
            vt[:, ri] = v[ri, :].T
            qb = q[ri, :]
            qh = q[hi, :]
            top = None
            for rj in olds:
                sj = dot(k[rj, :], qb, NT)
                if rj is lo:
                    sj = jnp.concatenate([jnp.where(seen, sj[:, :HALF], -1e30), sj[:, HALF:]], axis=1)
                s[rj, ri] = sj
                tj = jnp.max(sj, axis=0, keepdims=True)
                top = tj if top is None else jnp.maximum(top, tj)
            sh = jnp.where(seen, dot(k[hi, :], qh, NT), -1e30)
            s[hi, hi] = sh
            top = tail(top, lambda x: jnp.maximum(x, jnp.max(sh, axis=0, keepdims=True)))
            stages.append((lo, hi, ri, olds, qb, qh, top))
        later = []
        for lo, hi, ri, olds, qb, qh, top in stages:
            weight, acc = None, None
            for rj in olds:
                pj = jnp.exp2((s[rj, ri] - top) * (FACTOR * LOG2E))
                s[rj, ri] = pj
                lj = jnp.sum(pj, axis=0, keepdims=True)
                oj = dot(vt[:, rj], pj.astype(BF), NN)
                weight = lj if weight is None else weight + lj
                acc = oj if acc is None else acc + oj
            ph = jnp.exp2((s[hi, hi] - top[:, HALF:]) * (FACTOR * LOG2E))
            s[hi, hi] = ph
            weight = tail(weight, lambda x: x + jnp.sum(ph, axis=0, keepdims=True))
            acc = tail(acc, lambda x: x + dot(vt[:, hi], ph.astype(BF), NN))
            inverse = 1.0 / weight
            ob = (acc * inverse).astype(BF)
            gt = g[ri, :].T.astype(F32) * inverse
            gb = gt.astype(BF)
            delta = jnp.sum(gt * ob.astype(F32), axis=0, keepdims=True)
            acc = None
            for rj in olds:
                dp = dot(v[rj, :], gb, NN)
                pj = s[rj, ri]
                ds = (pj * (dp - delta)).astype(BF)
                vj = dot(pj.astype(BF), gb, NT)
                kj = dot(ds, qb, NN)
                if rj is lo:
                    dv[rj, :] = vj
                    dk[rj, :] = kj
                else:
                    dv[rj, :] += vj
                    dk[rj, :] += kj
                qj = dot(kt[:, rj], ds, NN)
                acc = qj if acc is None else acc + qj
            dp = dot(v[hi, :], gb[:, HALF:], NN)
            ph = s[hi, hi]
            ds = (ph * (dp - delta[:, HALF:])).astype(BF)
            dv[hi, :] = dot(ph.astype(BF), gb[:, HALF:], NT)
            dk[hi, :] = dot(ds, qh, NN)
            acc = tail(acc, lambda x: x + dot(kt[:, hi], ds, NN))
            q[ri, :] = (acc * FACTOR).astype(BF).T
            g[ri, :] = ob.T
        for dst, e, where in places(slots_out):
            dst[part(0, e), :] = g[where, :]
            dst[part(1, e), :] = q[where, :]
            dst[part(2, e), :] = (dk[where, :] * FACTOR).astype(BF)
            dst[part(3, e), :] = dv[where, :].astype(BF)


def pack_kernel(order, q, k, v, g, rest1, outer1, cross1, outer0, cross0, rest0, mine, turn, order_out, sem, order_sem):
    sh = q.shape[0]
    _, side, owner = place_here()
    turn[...] = jnp.zeros_like(turn)
    for core, outer, cross, rest in ((0, outer0, cross0, rest0), (1, outer1, cross1, rest1)):
        for held, halves in ((True, ((cross, 1 - side), (mine, side))), (False, ((rest, 1 - side), (outer, side)))):
            @pl.when((lax.axis_index("mp") == core) & (owner == held))
            def _():
                run_copies([
                    pltpu.make_async_copy(src.at[:, columns(half)], dst.at[n * sh:(n + 1) * sh, :], sem.at[m, n])
                    for m, (dst, half) in enumerate(halves)
                    for n, src in enumerate((q, k, v, g))
                ] + [pltpu.make_async_copy(order, order_out, order_sem)])


def unpack_kernel(own, r_a, r_c, r_b, *refs):
    outs, sem = refs[:4], refs[4]
    sh = outs[0].shape[0]
    me, side, _ = place_here()
    for at, near, far in ((0, r_a, r_c), (1, own, r_b), (2, own, r_b), (3, r_a, r_c)):
        @pl.when(me == at)
        def _():
            run_copies([
                pltpu.make_async_copy(src.at[n * sh:(n + 1) * sh, :], dst.at[:, columns(half)], sem.at[m, n])
                for m, (src, half) in enumerate(((far, 1 - side), (near, side)))
                for n, dst in enumerate(outs)
            ])


def in_vmem(*shapes):
    return tuple(pltpu.VMEM(shape, dtype) for shape, dtype in shapes)


def kept(*arrays):
    return tuple(pltpu.with_memory_space_constraint(x, pltpu.VMEM) for x in arrays)


def owned_per_device(span_order, queries, keys, values, grad_out):
    rows = queries.shape[0]
    total = 4 * rows
    anywhere = pl.BlockSpec(memory_space=pl.ANY)
    vm = pl.BlockSpec(memory_space=pltpu.VMEM)
    sm = pl.BlockSpec(memory_space=pltpu.SMEM)
    stack = ((4 * rows, HEAD_DIM), BF)
    per_row = ((total, HEAD_DIM), BF)
    per_column = ((HEAD_DIM, total), BF)
    wide = ((total, HEAD_DIM), F32)
    rest1, outer1, cross1, outer0, cross0, rest0, mine, turn, order = pl.pallas_call(
        pack_kernel,
        out_shape=in_vmem(*(stack,) * 7, ((16, HEAD_DIM), BF)) + (pltpu.SMEM(span_order.shape, span_order.dtype),),
        in_specs=[anywhere] * 5,
        out_specs=(vm,) * 8 + (sm,),
        scratch_shapes=[pltpu.SemaphoreType.DMA((2, 4)), pltpu.SemaphoreType.DMA],
        name="pack",
    )(span_order, queries, keys, values, grad_out)
    go = lambda x, pairs: lax.ppermute(x, "seq", pairs)

    def go_core(x, pairs, core):
        return lax.ppermute(x, ("seq", "mp"), [(2 * a + core, 2 * b + core) for a, b in pairs])

    g_c1 = go_core(rest1, [(0, 2), (3, 1)], 1)
    g_a1 = go_core(outer1, [(0, 1), (3, 2)], 1)
    g_b1 = go_core(cross1, [(1, 2), (2, 1)], 1)
    turn = lax.ppermute(turn, ("seq", "mp"), [(2 * a + 1, 2 * a + 0) for a in range(4)])
    outer0, cross0, rest0, turn = lax.optimization_barrier((outer0, cross0, rest0, turn))
    g_a0 = go_core(outer0, [(0, 1), (3, 2)], 0)
    g_c0 = go_core(rest0, [(0, 2), (3, 1)], 0)
    g_b0 = go_core(cross0, [(1, 2), (2, 1)], 0)
    own, to_a, to_c, to_b = pl.pallas_call(
        owner_kernel,
        out_shape=in_vmem(*(stack,) * 4),
        in_specs=[sm] + [vm] * 8,
        out_specs=(vm,) * 4,
        scratch_shapes=[
            *in_vmem(per_row, per_row, per_row, per_row, per_column, per_column, ((total, total), F32), wide, wide)
        ],
        compiler_params=pltpu.CompilerParams(vmem_limit_bytes=32 << 20),
        name="owner",
    )(order, *kept(turn, mine, g_c1, g_a1, g_b1, g_a0, g_c0, g_b0))
    r_a = go(to_a, [(1, 0), (2, 3)])
    r_b = go(to_b, [(1, 2), (2, 1)])
    r_c = go(to_c, [(1, 3), (2, 0)])
    return pl.pallas_call(
        unpack_kernel,
        out_shape=(jax.ShapeDtypeStruct(queries.shape, BF),) * 4,
        in_specs=[vm] * 4,
        out_specs=(anywhere,) * 4,
        scratch_shapes=[pltpu.SemaphoreType.DMA((2, 4))],
        name="unpack",
    )(*kept(own, r_a, r_c, r_b))


def solution(mesh):
    rows_columns = P(("groups", "seq"), ("head", "mp"))

    def run(span_order, queries, keys, values, grad_out):
        heads_here = queries.shape[1] // HEAD_DIM // (mesh.shape["head"] * mesh.shape["mp"])
        small = mesh.shape["seq"] == 4 and heads_here == 2
        return jax.shard_map(
            owned_per_device if small else gathered_per_device,
            mesh=mesh,
            in_specs=(P("groups"),) + (rows_columns,) * 4,
            out_specs=(rows_columns,) * 4,
            check_vma=False,
        )(span_order, queries, keys, values, grad_out)

    return run
```

```python
import functools

import jax
import jax.numpy as jnp
from jax import lax
from jax.experimental import pallas as pl
from jax.experimental.pallas import tpu as pltpu
from jax.sharding import PartitionSpec as P

HEAD_DIM = 128
SPAN = 128


def settle(values_in):
    return lax.optimization_barrier(values_in.astype(jnp.bfloat16)).astype(jnp.float32)


def masked_scores(query_block, key_block, query_pos, key_positions, factor):
    raw = (
        jnp.einsum("qhd,khd->hqk", query_block, key_block, preferred_element_type=jnp.float32)
        * factor
    )
    return jnp.where(key_positions[None, None, :] <= query_pos[None, :, None], raw, -jnp.inf)


def split_blocks(arrays, block_rows):
    count_blocks = arrays[0].shape[0] // block_rows
    stacked = tuple(
        (member.reshape((count_blocks, block_rows) + member.shape[1:]) for member in arrays)
    )
    starts = jnp.arange(count_blocks, dtype=jnp.int32) * block_rows
    return (stacked, starts)


def gathered_per_device(span_order, queries, keys, values, grad_out):
    q_rows, k_rows, v_rows, g_rows = (queries, keys, values, grad_out)
    my_rows = q_rows.shape[0]
    heads_here = q_rows.shape[1] // HEAD_DIM
    factor = HEAD_DIM ** (-0.5)
    total_rows = span_order.shape[0] * SPAN
    offsets = jnp.arange(total_rows, dtype=jnp.int32)
    all_pos = jnp.repeat(span_order, SPAN, total_repeat_length=total_rows) * SPAN + offsets % SPAN
    my_start = lax.axis_index("seq") * my_rows
    my_pos = lax.dynamic_slice_in_dim(all_pos, my_start, my_rows)
    my_q = q_rows.reshape(my_rows, heads_here, HEAD_DIM)
    my_k = k_rows.reshape(my_rows, heads_here, HEAD_DIM)
    my_v = v_rows.reshape(my_rows, heads_here, HEAD_DIM)
    my_g = g_rows.reshape(my_rows, heads_here, HEAD_DIM)

    def key_block_rows():
        return 512

    start_state = (
        jnp.full((heads_here, my_rows), -jnp.inf, jnp.float32),
        jnp.zeros((heads_here, my_rows), jnp.float32),
        jnp.zeros((heads_here, my_rows, HEAD_DIM), jnp.float32),
    )
    carry = start_state
    block_rows = key_block_rows()
    stacked, starts = split_blocks(
        (
            lax.all_gather(k_rows, "seq", axis=0, tiled=True),
            lax.all_gather(v_rows, "seq", axis=0, tiled=True),
        ),
        block_rows,
    )

    def forward_one_block(state, item):
        key_block, value_block, block_start = item
        key3 = key_block.reshape(block_rows, heads_here, HEAD_DIM)
        value3 = value_block.reshape(block_rows, heads_here, HEAD_DIM)
        positions = lax.dynamic_slice_in_dim(all_pos, block_start, block_rows)
        row_max, weight_sum, accum = state
        scores = masked_scores(my_q, key3, my_pos, positions, factor)
        new_max = jnp.maximum(row_max, jnp.max(scores, axis=2))
        safe_max = jnp.where(jnp.isfinite(new_max), new_max, 0.0)
        weights = jnp.exp(scores - safe_max[:, :, None])
        shrink = jnp.exp(row_max - safe_max)
        weight_sum = weight_sum * shrink + jnp.sum(weights, axis=2)
        accum = accum * shrink[:, :, None] + jnp.einsum(
            "hqk,khd->hqd", weights, value3.astype(jnp.float32)
        )
        return ((new_max, weight_sum, accum), None)

    carry, unused = lax.scan(forward_one_block, carry, stacked + (starts,))
    row_max, weight_sum, accum = carry
    lse_rows = (row_max + jnp.log(weight_sum)).T
    attended3 = jnp.transpose(accum / weight_sum[:, :, None], (1, 0, 2)).astype(jnp.bfloat16)
    delta_rows = jnp.sum(my_g.astype(jnp.float32) * attended3.astype(jnp.float32), axis=2)
    lse_all, delta_all = (
        lax.all_gather(lse_rows, "seq", axis=0, tiled=True),
        lax.all_gather(delta_rows, "seq", axis=0, tiled=True),
    )

    def pair_terms(
        q_block, g_block, lse_block, delta_block, q_pos, key_block, value_block, key_positions
    ):
        scores = masked_scores(q_block, key_block, q_pos, key_positions, factor)
        probs = jnp.exp(scores - lse_block.T[:, :, None])
        dprobs = jnp.einsum(
            "qhd,khd->hqk", g_block, value_block, preferred_element_type=jnp.float32
        )
        dscores = (probs * (dprobs - delta_block.T[:, :, None])).astype(jnp.bfloat16)
        return (probs.astype(jnp.bfloat16), dscores)

    def query_part(acc_q, key3, value3, positions):
        unused, dscores = pair_terms(
            my_q, my_g, lse_rows, delta_rows, my_pos, key3, value3, positions
        )
        return acc_q + jnp.einsum("hqk,khd->hqd", dscores, key3, preferred_element_type=jnp.float32)

    def key_part(acc_kv, q3, g3, block_start):
        positions = lax.dynamic_slice_in_dim(all_pos, block_start, my_rows)
        lse_block = lax.dynamic_slice_in_dim(lse_all, block_start, my_rows, 0)
        delta_block = lax.dynamic_slice_in_dim(delta_all, block_start, my_rows, 0)
        grad_k, grad_v = acc_kv
        probs_half, dscores = pair_terms(
            q3, g3, lse_block, delta_block, positions, my_k, my_v, my_pos
        )
        grad_k = grad_k + settle(
            jnp.einsum("hqk,qhd->khd", dscores, q3, preferred_element_type=jnp.float32) * factor
        )
        grad_v = grad_v + settle(
            jnp.einsum("hqk,qhd->khd", probs_half, g3, preferred_element_type=jnp.float32)
        )
        return (grad_k, grad_v)

    zeros_q = jnp.zeros((heads_here, my_rows, HEAD_DIM), jnp.float32)
    zeros_k = jnp.zeros((my_rows, heads_here, HEAD_DIM), jnp.float32)
    carry = zeros_q
    query_block_rows = key_block_rows()
    stacked, starts = split_blocks(
        (
            lax.all_gather(k_rows, "seq", axis=0, tiled=True),
            lax.all_gather(v_rows, "seq", axis=0, tiled=True),
        ),
        query_block_rows,
    )

    def query_one_block(state, item):
        key_block, value_block, block_start = item
        positions = lax.dynamic_slice_in_dim(all_pos, block_start, query_block_rows)
        key3 = key_block.reshape(query_block_rows, heads_here, HEAD_DIM)
        value3 = value_block.reshape(query_block_rows, heads_here, HEAD_DIM)
        return (query_part(state, key3, value3, positions), None)

    carry, unused = lax.scan(query_one_block, carry, stacked + (starts,))
    grad_q_acc = carry
    carry = (zeros_k, zeros_k)
    stacked, starts = split_blocks(
        (
            lax.all_gather(q_rows, "seq", axis=0, tiled=True),
            lax.all_gather(g_rows, "seq", axis=0, tiled=True),
        ),
        my_rows,
    )

    def key_one_block(state, item):
        query_block, cotangent_block, block_start = item
        q3 = query_block.reshape(my_rows, heads_here, HEAD_DIM)
        g3 = cotangent_block.reshape(my_rows, heads_here, HEAD_DIM)
        return (key_part(state, q3, g3, block_start), None)

    carry, unused = lax.scan(key_one_block, carry, stacked + (starts,))
    grad_k_acc, grad_v_acc = carry
    attended_rows = attended3.reshape(my_rows, heads_here * HEAD_DIM)
    grad_q_rows = (
        (jnp.transpose(grad_q_acc, (1, 0, 2)) * factor)
        .astype(jnp.bfloat16)
        .reshape(my_rows, heads_here * HEAD_DIM)
    )
    grad_k_rows = grad_k_acc.astype(jnp.bfloat16).reshape(my_rows, heads_here * HEAD_DIM)
    grad_v_rows = grad_v_acc.astype(jnp.bfloat16).reshape(my_rows, heads_here * HEAD_DIM)
    return (attended_rows, grad_q_rows, grad_k_rows, grad_v_rows)


F32 = jnp.float32
BF = jnp.bfloat16
NN = (((1,), (0,)), ((), ()))
NT = (((1,), (1,)), ((), ()))
LOG2E = 1.4426950408889634
FACTOR = HEAD_DIM**-0.5
BLOCK = 512
HALF = 256


def dot(a, b, dims):
    return lax.dot_general(a, b, dims, preferred_element_type=F32)


def place_here():
    me = lax.axis_index("seq")
    side = lax.div(me, 2)
    owner = (me == 1) | (me == 2)
    return me, side, owner


def columns(half):
    return pl.ds(pl.multiple_of(half * HEAD_DIM, HEAD_DIM), HEAD_DIM)


def run_copies(copies):
    for one in copies:
        one.start()
    for one in copies:
        one.wait()


def owner_kernel(order_ref, turn, own, s_c1, s_a1, s_b1, s_a0, s_c0, s_b0, o_own, o_a, o_c, o_b, q, k, v, g, kt, vt, s, dk, dv):
    me, side, held = place_here()
    rows = own.shape[0] // 4
    total = 4 * rows
    per = rows // SPAN
    near_at, far_at = 3 * side, 3 - 3 * side
    slots_out = ((me, o_own), (near_at, o_a), (far_at, o_c), (3 - me, o_b))

    @pl.when(held)
    def _():
        places = lambda slots: [
            (ref, e, pl.ds(pl.multiple_of(order_ref[at * per + e] * SPAN, SPAN), SPAN))
            for at, ref in slots
            for e in range(per)
        ]
        part = lambda n, e: slice(n * rows + e * SPAN, n * rows + (e + 1) * SPAN)
        def collect(slots):
            for src, e, where in places(slots):
                for n, to in enumerate((q, k, v, g)):
                    to[where, :] = src[part(n, e), :]

        for core, arrived in enumerate((
            ((me, own), (far_at, s_c0), (near_at, s_a0), (3 - me, s_b0)),
            ((me, own), (far_at, s_c1), (near_at, s_a1), (3 - me, s_b1)),
        )):
            pl.when(lax.axis_index("mp") == core)(functools.partial(collect, arrived))
        key_at = lax.broadcasted_iota(jnp.int32, (HALF, HALF), 0)
        query_at = lax.broadcasted_iota(jnp.int32, (HALF, HALF), 1)
        seen = key_at <= query_at
        tail = lambda whole, part: jnp.concatenate([whole[:, :HALF], part(whole[:, HALF:])], axis=1)
        stages = []
        for i in range(total // BLOCK):
            lo = slice(i * BLOCK, i * BLOCK + HALF)
            hi = slice(i * BLOCK + HALF, (i + 1) * BLOCK)
            ri = slice(i * BLOCK, (i + 1) * BLOCK)
            olds = [slice(j * BLOCK, (j + 1) * BLOCK) for j in range(i)] + [lo]
            qb = q[ri, :]
            qh = q[hi, :]
            top = None
            for rj in olds:
                sj = dot(k[rj, :], qb, NT)
                if rj is lo:
                    sj = jnp.concatenate([jnp.where(seen, sj[:, :HALF], -1e30), sj[:, HALF:]], axis=1)
                s[rj, ri] = sj
                tj = jnp.max(sj, axis=0, keepdims=True)
                top = tj if top is None else jnp.maximum(top, tj)
            sh = jnp.where(seen, dot(k[hi, :], qh, NT), -1e30)
            s[hi, hi] = sh
            top = tail(top, lambda x: jnp.maximum(x, jnp.max(sh, axis=0, keepdims=True)))
            stages.append((lo, hi, ri, olds, qb, qh, top))
        later = []
        for lo, hi, ri, olds, qb, qh, top in stages:
            kt[:, ri] = k[ri, :].T
            vt[:, ri] = v[ri, :].T
            weight, acc = None, None
            for rj in olds:
                pj = jnp.exp2((s[rj, ri] - top) * (FACTOR * LOG2E))
                s[rj, ri] = pj
                lj = jnp.sum(pj, axis=0, keepdims=True)
                oj = dot(vt[:, rj], pj.astype(BF), NN)
                weight = lj if weight is None else weight + lj
                acc = oj if acc is None else acc + oj
            ph = jnp.exp2((s[hi, hi] - top[:, HALF:]) * (FACTOR * LOG2E))
            s[hi, hi] = ph
            weight = tail(weight, lambda x: x + jnp.sum(ph, axis=0, keepdims=True))
            acc = tail(acc, lambda x: x + dot(vt[:, hi], ph.astype(BF), NN))
            inverse = 1.0 / weight
            ob = (acc * inverse).astype(BF)
            gt = g[ri, :].T.astype(F32) * inverse
            gb = gt.astype(BF)
            delta = jnp.sum(gt * ob.astype(F32), axis=0, keepdims=True)
            acc = None
            for rj in olds:
                dp = dot(v[rj, :], gb, NN)
                pj = s[rj, ri]
                ds = (pj * (dp - delta)).astype(BF)
                vj = dot(pj.astype(BF), gb, NT)
                kj = dot(ds, qb, NN)
                if rj is lo:
                    dv[rj, :] = vj
                    dk[rj, :] = kj
                else:
                    dv[rj, :] += vj
                    dk[rj, :] += kj
                qj = dot(kt[:, rj], ds, NN)
                acc = qj if acc is None else acc + qj
            dp = dot(v[hi, :], gb[:, HALF:], NN)
            ph = s[hi, hi]
            ds = (ph * (dp - delta[:, HALF:])).astype(BF)
            dv[hi, :] = dot(ph.astype(BF), gb[:, HALF:], NT)
            dk[hi, :] = dot(ds, qh, NN)
            acc = tail(acc, lambda x: x + dot(kt[:, hi], ds, NN))
            q[ri, :] = (acc * FACTOR).astype(BF).T
            g[ri, :] = ob.T
        for dst, e, where in places(slots_out):
            dst[part(0, e), :] = g[where, :]
            dst[part(1, e), :] = q[where, :]
            dst[part(2, e), :] = (dk[where, :] * FACTOR).astype(BF)
            dst[part(3, e), :] = dv[where, :].astype(BF)


def pack_kernel(order, q, k, v, g, rest1, outer1, cross1, outer0, cross0, rest0, mine, turn, order_out, sem, order_sem):
    sh = q.shape[0]
    _, side, owner = place_here()
    turn[...] = jnp.zeros_like(turn)
    for core, outer, cross, rest in ((0, outer0, cross0, rest0), (1, outer1, cross1, rest1)):
        for held, halves in ((True, ((cross, 1 - side), (mine, side))), (False, ((rest, 1 - side), (outer, side)))):
            @pl.when((lax.axis_index("mp") == core) & (owner == held))
            def _():
                run_copies([
                    pltpu.make_async_copy(src.at[:, columns(half)], dst.at[n * sh:(n + 1) * sh, :], sem.at[m, n])
                    for m, (dst, half) in enumerate(halves)
                    for n, src in enumerate((q, k, v, g))
                ] + [pltpu.make_async_copy(order, order_out, order_sem)])


def unpack_kernel(own, r_a, r_c, r_b, *refs):
    outs, sem = refs[:4], refs[4]
    sh = outs[0].shape[0]
    me, side, _ = place_here()
    for at, near, far in ((0, r_a, r_c), (1, own, r_b), (2, own, r_b), (3, r_a, r_c)):
        @pl.when(me == at)
        def _():
            run_copies([
                pltpu.make_async_copy(src.at[n * sh:(n + 1) * sh, :], dst.at[:, columns(half)], sem.at[m, n])
                for m, (src, half) in enumerate(((far, 1 - side), (near, side)))
                for n, dst in enumerate(outs)
            ])


def in_vmem(*shapes):
    return tuple(pltpu.VMEM(shape, dtype) for shape, dtype in shapes)


def kept(*arrays):
    return tuple(pltpu.with_memory_space_constraint(x, pltpu.VMEM) for x in arrays)


def owned_per_device(span_order, queries, keys, values, grad_out):
    rows = queries.shape[0]
    total = 4 * rows
    anywhere = pl.BlockSpec(memory_space=pl.ANY)
    vm = pl.BlockSpec(memory_space=pltpu.VMEM)
    sm = pl.BlockSpec(memory_space=pltpu.SMEM)
    stack = ((4 * rows, HEAD_DIM), BF)
    per_row = ((total, HEAD_DIM), BF)
    per_column = ((HEAD_DIM, total), BF)
    wide = ((total, HEAD_DIM), F32)
    rest1, outer1, cross1, outer0, cross0, rest0, mine, turn, order = pl.pallas_call(
        pack_kernel,
        out_shape=in_vmem(*(stack,) * 7, ((16, HEAD_DIM), BF)) + (pltpu.SMEM(span_order.shape, span_order.dtype),),
        in_specs=[anywhere] * 5,
        out_specs=(vm,) * 8 + (sm,),
        scratch_shapes=[pltpu.SemaphoreType.DMA((2, 4)), pltpu.SemaphoreType.DMA],
        name="pack",
    )(span_order, queries, keys, values, grad_out)
    go = lambda x, pairs: lax.ppermute(x, "seq", pairs)

    def go_core(x, pairs, core):
        return lax.ppermute(x, ("seq", "mp"), [(2 * a + core, 2 * b + core) for a, b in pairs])

    g_c1 = go_core(rest1, [(0, 2), (3, 1)], 1)
    g_a1 = go_core(outer1, [(0, 1), (3, 2)], 1)
    g_b1 = go_core(cross1, [(1, 2), (2, 1)], 1)
    turn = lax.ppermute(turn, ("seq", "mp"), [(2 * a + 1, 2 * a + 0) for a in range(4)])
    outer0, cross0, rest0, turn = lax.optimization_barrier((outer0, cross0, rest0, turn))
    g_a0 = go_core(outer0, [(0, 1), (3, 2)], 0)
    g_c0 = go_core(rest0, [(0, 2), (3, 1)], 0)
    g_b0 = go_core(cross0, [(1, 2), (2, 1)], 0)
    own, to_a, to_c, to_b = pl.pallas_call(
        owner_kernel,
        out_shape=in_vmem(*(stack,) * 4),
        in_specs=[sm] + [vm] * 8,
        out_specs=(vm,) * 4,
        scratch_shapes=[
            *in_vmem(per_row, per_row, per_row, per_row, per_column, per_column, ((total, total), F32), wide, wide)
        ],
        compiler_params=pltpu.CompilerParams(vmem_limit_bytes=32 << 20),
        name="owner",
    )(order, *kept(turn, mine, g_c1, g_a1, g_b1, g_a0, g_c0, g_b0))
    r_a = go(to_a, [(1, 0), (2, 3)])
    r_b = go(to_b, [(1, 2), (2, 1)])
    r_c = go(to_c, [(1, 3), (2, 0)])
    return pl.pallas_call(
        unpack_kernel,
        out_shape=(jax.ShapeDtypeStruct(queries.shape, BF),) * 4,
        in_specs=[vm] * 4,
        out_specs=(anywhere,) * 4,
        scratch_shapes=[pltpu.SemaphoreType.DMA((2, 4))],
        name="unpack",
    )(*kept(own, r_a, r_c, r_b))


def solution(mesh):
    rows_columns = P(("groups", "seq"), ("head", "mp"))

    def run(span_order, queries, keys, values, grad_out):
        heads_here = queries.shape[1] // HEAD_DIM // (mesh.shape["head"] * mesh.shape["mp"])
        small = mesh.shape["seq"] == 4 and heads_here == 2
        return jax.shard_map(
            owned_per_device if small else gathered_per_device,
            mesh=mesh,
            in_specs=(P("groups"),) + (rows_columns,) * 4,
            out_specs=(rows_columns,) * 4,
            check_vma=False,
        )(span_order, queries, keys, values, grad_out)

    return run
```

```python
import functools

import jax
import jax.numpy as jnp
from jax import lax
from jax.experimental import pallas as pl
from jax.experimental.pallas import tpu as pltpu
from jax.sharding import PartitionSpec as P

HEAD_DIM = 128
SPAN = 128


def settle(values_in):
    return lax.optimization_barrier(values_in.astype(jnp.bfloat16)).astype(jnp.float32)


def masked_scores(query_block, key_block, query_pos, key_positions, factor):
    raw = (
        jnp.einsum("qhd,khd->hqk", query_block, key_block, preferred_element_type=jnp.float32)
        * factor
    )
    return jnp.where(key_positions[None, None, :] <= query_pos[None, :, None], raw, -jnp.inf)


def split_blocks(arrays, block_rows):
    count_blocks = arrays[0].shape[0] // block_rows
    stacked = tuple(
        (member.reshape((count_blocks, block_rows) + member.shape[1:]) for member in arrays)
    )
    starts = jnp.arange(count_blocks, dtype=jnp.int32) * block_rows
    return (stacked, starts)


def gathered_per_device(span_order, queries, keys, values, grad_out):
    q_rows, k_rows, v_rows, g_rows = (queries, keys, values, grad_out)
    my_rows = q_rows.shape[0]
    heads_here = q_rows.shape[1] // HEAD_DIM
    factor = HEAD_DIM ** (-0.5)
    total_rows = span_order.shape[0] * SPAN
    offsets = jnp.arange(total_rows, dtype=jnp.int32)
    all_pos = jnp.repeat(span_order, SPAN, total_repeat_length=total_rows) * SPAN + offsets % SPAN
    my_start = lax.axis_index("seq") * my_rows
    my_pos = lax.dynamic_slice_in_dim(all_pos, my_start, my_rows)
    my_q = q_rows.reshape(my_rows, heads_here, HEAD_DIM)
    my_k = k_rows.reshape(my_rows, heads_here, HEAD_DIM)
    my_v = v_rows.reshape(my_rows, heads_here, HEAD_DIM)
    my_g = g_rows.reshape(my_rows, heads_here, HEAD_DIM)

    def key_block_rows():
        return 512

    start_state = (
        jnp.full((heads_here, my_rows), -jnp.inf, jnp.float32),
        jnp.zeros((heads_here, my_rows), jnp.float32),
        jnp.zeros((heads_here, my_rows, HEAD_DIM), jnp.float32),
    )
    carry = start_state
    block_rows = key_block_rows()
    stacked, starts = split_blocks(
        (
            lax.all_gather(k_rows, "seq", axis=0, tiled=True),
            lax.all_gather(v_rows, "seq", axis=0, tiled=True),
        ),
        block_rows,
    )

    def forward_one_block(state, item):
        key_block, value_block, block_start = item
        key3 = key_block.reshape(block_rows, heads_here, HEAD_DIM)
        value3 = value_block.reshape(block_rows, heads_here, HEAD_DIM)
        positions = lax.dynamic_slice_in_dim(all_pos, block_start, block_rows)
        row_max, weight_sum, accum = state
        scores = masked_scores(my_q, key3, my_pos, positions, factor)
        new_max = jnp.maximum(row_max, jnp.max(scores, axis=2))
        safe_max = jnp.where(jnp.isfinite(new_max), new_max, 0.0)
        weights = jnp.exp(scores - safe_max[:, :, None])
        shrink = jnp.exp(row_max - safe_max)
        weight_sum = weight_sum * shrink + jnp.sum(weights, axis=2)
        accum = accum * shrink[:, :, None] + jnp.einsum(
            "hqk,khd->hqd", weights, value3.astype(jnp.float32)
        )
        return ((new_max, weight_sum, accum), None)

    carry, unused = lax.scan(forward_one_block, carry, stacked + (starts,))
    row_max, weight_sum, accum = carry
    lse_rows = (row_max + jnp.log(weight_sum)).T
    attended3 = jnp.transpose(accum / weight_sum[:, :, None], (1, 0, 2)).astype(jnp.bfloat16)
    delta_rows = jnp.sum(my_g.astype(jnp.float32) * attended3.astype(jnp.float32), axis=2)
    lse_all, delta_all = (
        lax.all_gather(lse_rows, "seq", axis=0, tiled=True),
        lax.all_gather(delta_rows, "seq", axis=0, tiled=True),
    )

    def pair_terms(
        q_block, g_block, lse_block, delta_block, q_pos, key_block, value_block, key_positions
    ):
        scores = masked_scores(q_block, key_block, q_pos, key_positions, factor)
        probs = jnp.exp(scores - lse_block.T[:, :, None])
        dprobs = jnp.einsum(
            "qhd,khd->hqk", g_block, value_block, preferred_element_type=jnp.float32
        )
        dscores = (probs * (dprobs - delta_block.T[:, :, None])).astype(jnp.bfloat16)
        return (probs.astype(jnp.bfloat16), dscores)

    def query_part(acc_q, key3, value3, positions):
        unused, dscores = pair_terms(
            my_q, my_g, lse_rows, delta_rows, my_pos, key3, value3, positions
        )
        return acc_q + jnp.einsum("hqk,khd->hqd", dscores, key3, preferred_element_type=jnp.float32)

    def key_part(acc_kv, q3, g3, block_start):
        positions = lax.dynamic_slice_in_dim(all_pos, block_start, my_rows)
        lse_block = lax.dynamic_slice_in_dim(lse_all, block_start, my_rows, 0)
        delta_block = lax.dynamic_slice_in_dim(delta_all, block_start, my_rows, 0)
        grad_k, grad_v = acc_kv
        probs_half, dscores = pair_terms(
            q3, g3, lse_block, delta_block, positions, my_k, my_v, my_pos
        )
        grad_k = grad_k + settle(
            jnp.einsum("hqk,qhd->khd", dscores, q3, preferred_element_type=jnp.float32) * factor
        )
        grad_v = grad_v + settle(
            jnp.einsum("hqk,qhd->khd", probs_half, g3, preferred_element_type=jnp.float32)
        )
        return (grad_k, grad_v)

    zeros_q = jnp.zeros((heads_here, my_rows, HEAD_DIM), jnp.float32)
    zeros_k = jnp.zeros((my_rows, heads_here, HEAD_DIM), jnp.float32)
    carry = zeros_q
    query_block_rows = key_block_rows()
    stacked, starts = split_blocks(
        (
            lax.all_gather(k_rows, "seq", axis=0, tiled=True),
            lax.all_gather(v_rows, "seq", axis=0, tiled=True),
        ),
        query_block_rows,
    )

    def query_one_block(state, item):
        key_block, value_block, block_start = item
        positions = lax.dynamic_slice_in_dim(all_pos, block_start, query_block_rows)
        key3 = key_block.reshape(query_block_rows, heads_here, HEAD_DIM)
        value3 = value_block.reshape(query_block_rows, heads_here, HEAD_DIM)
        return (query_part(state, key3, value3, positions), None)

    carry, unused = lax.scan(query_one_block, carry, stacked + (starts,))
    grad_q_acc = carry
    carry = (zeros_k, zeros_k)
    stacked, starts = split_blocks(
        (
            lax.all_gather(q_rows, "seq", axis=0, tiled=True),
            lax.all_gather(g_rows, "seq", axis=0, tiled=True),
        ),
        my_rows,
    )

    def key_one_block(state, item):
        query_block, cotangent_block, block_start = item
        q3 = query_block.reshape(my_rows, heads_here, HEAD_DIM)
        g3 = cotangent_block.reshape(my_rows, heads_here, HEAD_DIM)
        return (key_part(state, q3, g3, block_start), None)

    carry, unused = lax.scan(key_one_block, carry, stacked + (starts,))
    grad_k_acc, grad_v_acc = carry
    attended_rows = attended3.reshape(my_rows, heads_here * HEAD_DIM)
    grad_q_rows = (
        (jnp.transpose(grad_q_acc, (1, 0, 2)) * factor)
        .astype(jnp.bfloat16)
        .reshape(my_rows, heads_here * HEAD_DIM)
    )
    grad_k_rows = grad_k_acc.astype(jnp.bfloat16).reshape(my_rows, heads_here * HEAD_DIM)
    grad_v_rows = grad_v_acc.astype(jnp.bfloat16).reshape(my_rows, heads_here * HEAD_DIM)
    return (attended_rows, grad_q_rows, grad_k_rows, grad_v_rows)


F32 = jnp.float32
BF = jnp.bfloat16
NN = (((1,), (0,)), ((), ()))
NT = (((1,), (1,)), ((), ()))
LOG2E = 1.4426950408889634
FACTOR = HEAD_DIM**-0.5
BLOCK = 512
HALF = 256


def dot(a, b, dims):
    return lax.dot_general(a, b, dims, preferred_element_type=F32)


def place_here():
    me = lax.axis_index("seq")
    side = lax.div(me, 2)
    owner = (me == 1) | (me == 2)
    return me, side, owner


def columns(half):
    return pl.ds(pl.multiple_of(half * HEAD_DIM, HEAD_DIM), HEAD_DIM)


def run_copies(copies):
    for one in copies:
        one.start()
    for one in copies:
        one.wait()


def owner_kernel(order_ref, turn, own, s_c1, s_a1, s_b1, s_a0, s_c0, s_b0, o_own, o_a, o_c, o_b, q, k, v, g, kt, vt, s, dk, dv):
    me, side, held = place_here()
    rows = own.shape[0] // 4
    total = 4 * rows
    per = rows // SPAN
    near_at, far_at = 3 * side, 3 - 3 * side
    slots_out = ((me, o_own), (near_at, o_a), (far_at, o_c), (3 - me, o_b))

    @pl.when(held)
    def _():
        places = lambda slots: [
            (ref, e, pl.ds(pl.multiple_of(order_ref[at * per + e] * SPAN, SPAN), SPAN))
            for at, ref in slots
            for e in range(per)
        ]
        part = lambda n, e: slice(n * rows + e * SPAN, n * rows + (e + 1) * SPAN)
        def collect(slots):
            for src, e, where in places(slots):
                for n, to in enumerate((q, k, v, g)):
                    to[where, :] = src[part(n, e), :]

        for core, arrived in enumerate((
            ((me, own), (far_at, s_c0), (near_at, s_a0), (3 - me, s_b0)),
            ((me, own), (far_at, s_c1), (near_at, s_a1), (3 - me, s_b1)),
        )):
            pl.when(lax.axis_index("mp") == core)(functools.partial(collect, arrived))
        key_at = lax.broadcasted_iota(jnp.int32, (HALF, HALF), 0)
        query_at = lax.broadcasted_iota(jnp.int32, (HALF, HALF), 1)
        seen = key_at <= query_at
        tail = lambda whole, part: jnp.concatenate([whole[:, :HALF], part(whole[:, HALF:])], axis=1)
        stages = []
        for i in range(total // BLOCK):
            lo = slice(i * BLOCK, i * BLOCK + HALF)
            hi = slice(i * BLOCK + HALF, (i + 1) * BLOCK)
            ri = slice(i * BLOCK, (i + 1) * BLOCK)
            olds = [slice(j * BLOCK, (j + 1) * BLOCK) for j in range(i)] + [lo]
            qb = q[ri, :]
            qh = q[hi, :]
            top = None
            for rj in olds:
                sj = dot(k[rj, :], qb, NT)
                if rj is lo:
                    sj = jnp.concatenate([jnp.where(seen, sj[:, :HALF], -1e30), sj[:, HALF:]], axis=1)
                s[rj, ri] = sj
                tj = jnp.max(sj, axis=0, keepdims=True)
                top = tj if top is None else jnp.maximum(top, tj)
            sh = jnp.where(seen, dot(k[hi, :], qh, NT), -1e30)
            s[hi, hi] = sh
            top = tail(top, lambda x: jnp.maximum(x, jnp.max(sh, axis=0, keepdims=True)))
            stages.append((lo, hi, ri, olds, qb, qh, top))
        later = []
        for lo, hi, ri, olds, qb, qh, top in stages:
            kt[:, ri] = k[ri, :].T
            vt[:, ri] = v[ri, :].T
            weight, acc = None, None
            for rj in olds:
                pj = jnp.exp2((s[rj, ri] - top) * (FACTOR * LOG2E))
                s[rj, ri] = pj
                lj = jnp.sum(pj, axis=0, keepdims=True)
                oj = dot(vt[:, rj], pj.astype(BF), NN)
                weight = lj if weight is None else weight + lj
                acc = oj if acc is None else acc + oj
            ph = jnp.exp2((s[hi, hi] - top[:, HALF:]) * (FACTOR * LOG2E))
            s[hi, hi] = ph
            weight = tail(weight, lambda x: x + jnp.sum(ph, axis=0, keepdims=True))
            acc = tail(acc, lambda x: x + dot(vt[:, hi], ph.astype(BF), NN))
            inverse = 1.0 / weight
            ob = (acc * inverse).astype(BF)
            gt = g[ri, :].T.astype(F32) * inverse
            gb = gt.astype(BF)
            delta = jnp.sum(gt * ob.astype(F32), axis=0, keepdims=True)
            acc = None
            for rj in olds:
                dp = dot(v[rj, :], gb, NN)
                pj = s[rj, ri]
                vj = dot(pj.astype(BF), gb, NT)
                ds = (pj * (dp - delta)).astype(BF)
                kj = dot(ds, qb, NN)
                if rj is lo:
                    dv[rj, :] = vj
                    dk[rj, :] = kj
                else:
                    dv[rj, :] += vj
                    dk[rj, :] += kj
                qj = dot(kt[:, rj], ds, NN)
                acc = qj if acc is None else acc + qj
            dp = dot(v[hi, :], gb[:, HALF:], NN)
            ph = s[hi, hi]
            ds = (ph * (dp - delta[:, HALF:])).astype(BF)
            dv[hi, :] = dot(ph.astype(BF), gb[:, HALF:], NT)
            dk[hi, :] = dot(ds, qh, NN)
            acc = tail(acc, lambda x: x + dot(kt[:, hi], ds, NN))
            q[ri, :] = (acc * FACTOR).astype(BF).T
            g[ri, :] = ob.T
        for dst, e, where in places(slots_out):
            dst[part(0, e), :] = g[where, :]
            dst[part(1, e), :] = q[where, :]
            dst[part(2, e), :] = (dk[where, :] * FACTOR).astype(BF)
            dst[part(3, e), :] = dv[where, :].astype(BF)


def pack_kernel(order, q, k, v, g, rest1, outer1, cross1, outer0, cross0, rest0, mine, turn, order_out, sem, order_sem):
    sh = q.shape[0]
    _, side, owner = place_here()
    turn[...] = jnp.zeros_like(turn)
    for core, outer, cross, rest in ((0, outer0, cross0, rest0), (1, outer1, cross1, rest1)):
        for held, halves in ((True, ((cross, 1 - side), (mine, side))), (False, ((rest, 1 - side), (outer, side)))):
            @pl.when((lax.axis_index("mp") == core) & (owner == held))
            def _():
                run_copies([
                    pltpu.make_async_copy(src.at[:, columns(half)], dst.at[n * sh:(n + 1) * sh, :], sem.at[m, n])
                    for m, (dst, half) in enumerate(halves)
                    for n, src in enumerate((q, k, v, g))
                ] + [pltpu.make_async_copy(order, order_out, order_sem)])


def unpack_kernel(own, r_a, r_c, r_b, *refs):
    outs, sem = refs[:4], refs[4]
    sh = outs[0].shape[0]
    me, side, _ = place_here()
    for at, near, far in ((0, r_a, r_c), (1, own, r_b), (2, own, r_b), (3, r_a, r_c)):
        @pl.when(me == at)
        def _():
            run_copies([
                pltpu.make_async_copy(src.at[n * sh:(n + 1) * sh, :], dst.at[:, columns(half)], sem.at[m, n])
                for m, (src, half) in enumerate(((far, 1 - side), (near, side)))
                for n, dst in enumerate(outs)
            ])


def in_vmem(*shapes):
    return tuple(pltpu.VMEM(shape, dtype) for shape, dtype in shapes)


def kept(*arrays):
    return tuple(pltpu.with_memory_space_constraint(x, pltpu.VMEM) for x in arrays)


def owned_per_device(span_order, queries, keys, values, grad_out):
    rows = queries.shape[0]
    total = 4 * rows
    anywhere = pl.BlockSpec(memory_space=pl.ANY)
    vm = pl.BlockSpec(memory_space=pltpu.VMEM)
    sm = pl.BlockSpec(memory_space=pltpu.SMEM)
    stack = ((4 * rows, HEAD_DIM), BF)
    per_row = ((total, HEAD_DIM), BF)
    per_column = ((HEAD_DIM, total), BF)
    wide = ((total, HEAD_DIM), F32)
    rest1, outer1, cross1, outer0, cross0, rest0, mine, turn, order = pl.pallas_call(
        pack_kernel,
        out_shape=in_vmem(*(stack,) * 7, ((16, HEAD_DIM), BF)) + (pltpu.SMEM(span_order.shape, span_order.dtype),),
        in_specs=[anywhere] * 5,
        out_specs=(vm,) * 8 + (sm,),
        scratch_shapes=[pltpu.SemaphoreType.DMA((2, 4)), pltpu.SemaphoreType.DMA],
        name="pack",
    )(span_order, queries, keys, values, grad_out)
    go = lambda x, pairs: lax.ppermute(x, "seq", pairs)

    def go_core(x, pairs, core):
        return lax.ppermute(x, ("seq", "mp"), [(2 * a + core, 2 * b + core) for a, b in pairs])

    g_c1 = go_core(rest1, [(0, 2), (3, 1)], 1)
    g_a1 = go_core(outer1, [(0, 1), (3, 2)], 1)
    g_b1 = go_core(cross1, [(1, 2), (2, 1)], 1)
    turn = lax.ppermute(turn, ("seq", "mp"), [(2 * a + 1, 2 * a + 0) for a in range(4)])
    outer0, cross0, rest0, turn = lax.optimization_barrier((outer0, cross0, rest0, turn))
    g_a0 = go_core(outer0, [(0, 1), (3, 2)], 0)
    g_c0 = go_core(rest0, [(0, 2), (3, 1)], 0)
    g_b0 = go_core(cross0, [(1, 2), (2, 1)], 0)
    own, to_a, to_c, to_b = pl.pallas_call(
        owner_kernel,
        out_shape=in_vmem(*(stack,) * 4),
        in_specs=[sm] + [vm] * 8,
        out_specs=(vm,) * 4,
        scratch_shapes=[
            *in_vmem(per_row, per_row, per_row, per_row, per_column, per_column, ((total, total), F32), wide, wide)
        ],
        compiler_params=pltpu.CompilerParams(vmem_limit_bytes=32 << 20),
        name="owner",
    )(order, *kept(turn, mine, g_c1, g_a1, g_b1, g_a0, g_c0, g_b0))
    r_a = go(to_a, [(1, 0), (2, 3)])
    r_b = go(to_b, [(1, 2), (2, 1)])
    r_c = go(to_c, [(1, 3), (2, 0)])
    return pl.pallas_call(
        unpack_kernel,
        out_shape=(jax.ShapeDtypeStruct(queries.shape, BF),) * 4,
        in_specs=[vm] * 4,
        out_specs=(anywhere,) * 4,
        scratch_shapes=[pltpu.SemaphoreType.DMA((2, 4))],
        name="unpack",
    )(*kept(own, r_a, r_c, r_b))


def solution(mesh):
    rows_columns = P(("groups", "seq"), ("head", "mp"))

    def run(span_order, queries, keys, values, grad_out):
        heads_here = queries.shape[1] // HEAD_DIM // (mesh.shape["head"] * mesh.shape["mp"])
        small = mesh.shape["seq"] == 4 and heads_here == 2
        return jax.shard_map(
            owned_per_device if small else gathered_per_device,
            mesh=mesh,
            in_specs=(P("groups"),) + (rows_columns,) * 4,
            out_specs=(rows_columns,) * 4,
            check_vma=False,
        )(span_order, queries, keys, values, grad_out)

    return run
```
